128 devices in a mesh: wide: 16 (over z, x), narrow: 8 (over y, core).
Axes of the slice: x: 4, y: 4, z: 4, core: 2. Of those that a mesh axis runs over, the one named last changes fastest.
Arguments:
- design: float32 [262144, 128], P(('wide', 'narrow')), may hold values from 0.05 to 1
- filter_tiles: float32 [5, 128, 128], replicated
- filter_cols: int32 [262144, 5], P(('wide', 'narrow')), may hold values from -1 to 262143, as said below
- slot_block: int32 [262144], P(('wide', 'narrow')), may hold values from 0 to 262143, as said below
- holes: int32 [2048, 16384], P('wide', 'narrow'), may hold values 0 or 1
- squeeze_source: float32 [2048, 16384], P('wide', 'narrow'), may hold values from -6 to 6
- force_weight: float32 [2048, 16384], P('wide', 'narrow'), may hold values from 0.2 to 2
Outputs:
- pressure: float32 [2048, 16384], P('wide', 'narrow')
- sensitivity: float32 [262144, 128], P(('wide', 'narrow'))
The draws below stay inside these ranges and needn't reach their ends.
Inputs may be any that keep to these rules, and one draw needn't show every extreme that they name: `slot_block`: film blocks are ordered along a curve that visits the tiles in order and, inside a tile of 16 x 128 blocks, the blocks in Morton order (column bit lowest); for one stagger h with 512 <= h <= 1536, design slot s controls the block at curve position (s + h) mod 262144. So the slots of owner d (slots d * 2048 to (d + 1) * 2048 - 1) lie in tiles d and d + 1, those of the last owner in its own tile and tile 0. filter_cols[r, 0] = r; entries 1 to 4 are the design slots of the film blocks above, below, left and right of the block of slot r inside the same tile, -1 where that neighbour lies outside the tile.
All inputs are finite; a program needn't handle non-finite values. No bound on the sum of `holes` on one device may be relied on, other than what follows from the above.
Results may differ from the reference program's by a relative error of at most 0.00025.
Values sent between devices are 32-bit elements; how exact they have to be, the bound alone decides.
No kernel may reach another device: no remote copies, remote signals or barrier semaphores. Data moves between devices by JAX's collectives and lax.ppermute only.
A program may use at most 192 MiB of HBM per device.

```python
import math
import jax
import jax.numpy as jnp
from jax import lax

CR = 128
CC = 2048
SWEEPS = 16
KNB = 5
BLOCK = 128
SLOTS = 2048
NB = 262144
NR = 2048
NC = 16384
N_WIDE = 16
N_NARROW = 8


def draw_filter_tiles(key, part):
    logs = jax.random.uniform(jax.random.fold_in(key, 11), (KNB, 128, 128), jnp.float32, jnp.log(0.02), jnp.log(0.5))
    tiles = jnp.exp(logs) * (2.0 / 128.0)
    identity = jnp.eye(128, dtype=jnp.float32)
    return tiles.at[0].add(identity)


def stagger_of(key):
    return jax.random.randint(jax.random.fold_in(key, 41), (), SLOTS // 4, 3 * SLOTS // 4 + 1).astype(jnp.int32)


def bit_widths():
    return ((CR // 8).bit_length() - 1, (CC // 16).bit_length() - 1)


def decode_inner(inner):
    row_bits, col_bits = bit_widths()
    shared = min(row_bits, col_bits)
    block_row = jnp.zeros_like(inner)
    block_col = jnp.zeros_like(inner)
    place = 0
    for level in range(shared):
        block_col = block_col + inner // 2 ** place % 2 * 2 ** level
        place = place + 1
        block_row = block_row + inner // 2 ** place % 2 * 2 ** level
        place = place + 1
    for level in range(shared, row_bits):
        block_row = block_row + inner // 2 ** place % 2 * 2 ** level
        place = place + 1
    for level in range(shared, col_bits):
        block_col = block_col + inner // 2 ** place % 2 * 2 ** level
        place = place + 1
    return (block_row, block_col)


def encode_inner(block_row, block_col):
    row_bits, col_bits = bit_widths()
    shared = min(row_bits, col_bits)
    inner = jnp.zeros_like(block_row)
    place = 0
    for level in range(shared):
        inner = inner + block_col // 2 ** level % 2 * 2 ** place
        place = place + 1
        inner = inner + block_row // 2 ** level % 2 * 2 ** place
        place = place + 1
    for level in range(shared, row_bits):
        inner = inner + block_row // 2 ** level % 2 * 2 ** place
        place = place + 1
    for level in range(shared, col_bits):
        inner = inner + block_col // 2 ** level % 2 * 2 ** place
        place = place + 1
    return inner


def draw_slot_block(key, part):
    slots_all = jnp.arange(NB, dtype=jnp.int32)
    position = (slots_all + stagger_of(key)) % NB
    tile = position // SLOTS
    block_row, block_col = decode_inner(position % SLOTS)
    return (tile * SLOTS + block_row * (CC // 16) + block_col).astype(jnp.int32)


def draw_filter_cols(key, part):
    shift = stagger_of(key)
    slots_all = jnp.arange(NB, dtype=jnp.int32)
    position = (slots_all + shift) % NB
    tile = position // SLOTS
    block_row, block_col = decode_inner(position % SLOTS)
    columns = [slots_all]
    for row_step, col_step in ((-1, 0), (1, 0), (0, -1), (0, 1)):
        near_row = block_row + row_step
        near_col = block_col + col_step
        inside = (near_row >= 0) & (near_row < CR // 8) & (near_col >= 0) & (near_col < CC // 16)
        safe_row = jnp.clip(near_row, 0, CR // 8 - 1)
        safe_col = jnp.clip(near_col, 0, CC // 16 - 1)
        near_position = tile * SLOTS + encode_inner(safe_row, safe_col)
        near_slot = (near_position - shift + NB) % NB
        columns.append(jnp.where(inside, near_slot, -1))
    return jnp.stack(columns, axis=1).astype(jnp.int32)


def place_ends(values, rng, smallest, high):
    longest = values.shape.index(max(values.shape))
    spots = []
    for shift in (0, 1):
        where = [jax.random.randint(jax.random.fold_in(rng, axis), (), 0, length) for axis, length in enumerate(values.shape)]
        where[longest] = (where[longest] + shift) % values.shape[longest]
        spots.append(tuple(where))
    return values.at[spots[0]].set(smallest).at[spots[1]].set(high)


def shard_levels(own_key, dims, shards, low, top_value):
    def one(axis_at, parts):
        steps = jax.random.uniform(jax.random.fold_in(jax.random.fold_in(own_key, 6), axis_at), (parts,), jnp.float32, low / len(shards), top_value / len(shards))
        return jnp.repeat(jnp.exp(steps), dims[axis_at] // parts).reshape((-1,) + (1,) * (len(dims) - axis_at - 1))

    factor_of = one(*shards[0])
    for cut in shards[1:]:
        factor_of = factor_of * one(*cut)
    return factor_of


def bell_draw(own_key, extent, width, bound, shards=(), held_as=jnp.bfloat16):
    loudness = shard_levels(own_key, extent, shards, -0.22, 0.18) if shards else 1.0
    values = jax.random.normal(own_key, extent, jnp.float32) * width * loudness
    return jnp.minimum(jnp.maximum(values, -bound), bound).astype(held_as)


def setup_inputs(seed: int = 0) -> dict:
    keys = jax.random.split(jax.random.key(seed), 8)
    design = jnp.clip(0.05 + 0.95 * jax.random.uniform(keys[0], (NB, BLOCK), jnp.float32) ** shard_levels(keys[0], (NB, BLOCK), ((0, 128),), -0.2, 0.2), 0.05, 1.0)
    filter_tiles = draw_filter_tiles(jax.random.fold_in(keys[7], 71), 0)
    filter_cols = draw_filter_cols(jax.random.fold_in(keys[7], 71), 0)
    slot_block = draw_slot_block(jax.random.fold_in(keys[7], 71), 0)
    holes = place_ends((jax.random.randint(keys[4], (NR, NC), 0, 8) < 1).astype(jnp.int32), jax.random.fold_in(keys[4], 1), 0, 1)
    squeeze_source = bell_draw(keys[5], (NR, NC), 1.0, 6.0, ((0, 16), (1, 8)), jnp.float32)
    force_weight = jnp.clip(jnp.exp(math.log(2.0) - 2.3025851 * jax.random.uniform(keys[6], (NR, NC), jnp.float32) ** shard_levels(keys[6], (NR, NC), ((0, 16), (1, 8)), -0.2, 0.2)), 0.2, 2.0)
    return {"design": design, "filter_tiles": filter_tiles, "filter_cols": filter_cols, "slot_block": slot_block, "holes": holes, "squeeze_source": squeeze_source, "force_weight": force_weight}


COND_FLOOR = 0.01
SQUEEZE_DAMPING = 0.25
FULL_PRECISION = lax.Precision.HIGHEST


def relax(fields, conduct, sources, solid_mask, rim_depth, outer_rim):
    offset = outer_rim - rim_depth + 1
    inner_rows = fields.shape[1] - 2
    inner_cols = fields.shape[2] - 2

    def window(values, row_step, col_step):
        return values[..., offset + row_step:offset + row_step + inner_rows, offset + col_step:offset + col_step + inner_cols]

    k_here = window(conduct, 0, 0)
    face_north = 0.5 * (k_here + window(conduct, -1, 0))
    face_south = 0.5 * (k_here + window(conduct, 1, 0))
    face_west = 0.5 * (k_here + window(conduct, 0, -1))
    face_east = 0.5 * (k_here + window(conduct, 0, 1))
    coupled = face_north * fields[:, 0:inner_rows, 1:inner_cols + 1]
    coupled = coupled + face_south * fields[:, 2:inner_rows + 2, 1:inner_cols + 1]
    coupled = coupled + face_west * fields[:, 1:inner_rows + 1, 0:inner_cols]
    coupled = coupled + face_east * fields[:, 1:inner_rows + 1, 2:inner_cols + 2]
    diagonal = face_north + face_south + face_west + face_east + SQUEEZE_DAMPING
    return (window(sources, 0, 0) + coupled) / diagonal * window(solid_mask, 0, 0)


def film_gradient(padded, density):
    row_count = padded.shape[1] - 2
    col_count = padded.shape[2] - 2
    p_here = padded[0, 1:row_count + 1, 1:col_count + 1]
    a_here = padded[1, 1:row_count + 1, 1:col_count + 1]
    summed = jnp.zeros((row_count, col_count), jnp.float32)
    for row_start, col_start in ((0, 1), (2, 1), (1, 0), (1, 2)):
        nearby = padded[:, row_start:row_start + row_count, col_start:col_start + col_count]
        summed = summed + (a_here - nearby[1]) * (p_here - nearby[0])
    return -0.5 * summed * (3.0 * (1.0 - COND_FLOOR)) * density * density


def reference(design, filter_tiles, filter_cols, slot_block, holes, squeeze_source, force_weight):
    present = filter_cols >= 0
    safe_cols = jnp.where(present, filter_cols, 0).astype(jnp.int32)
    picked = jnp.where(present[:, :, None], design[safe_cols], 0.0)
    numer = jnp.einsum('rkj,kij->ri', picked, filter_tiles, precision=FULL_PRECISION)
    denom = jnp.dot(present.astype(jnp.float32), jnp.sum(filter_tiles, axis=2), precision=FULL_PRECISION)
    filtered = numer / denom
    placed = jnp.zeros((NB, 128), jnp.float32).at[slot_block].set(filtered)
    density = placed.reshape(N_WIDE, N_NARROW, CR // 8, CC // 16, 8, 16).transpose(0, 2, 4, 1, 3, 5).reshape(NR, NC)
    conduct = COND_FLOOR + (1.0 - COND_FLOOR) * density * density * density
    solid_mask = jnp.where(holes > 0, 0.0, 1.0).astype(jnp.float32)
    sources = jnp.stack([squeeze_source, force_weight])
    conduct_pad = jnp.pad(conduct, 1)
    sources_pad = jnp.pad(sources, ((0, 0), (1, 1), (1, 1)))
    solid_pad = jnp.pad(solid_mask, 1)
    fields = jnp.zeros((2, NR, NC), jnp.float32)
    for sweep_index in range(SWEEPS):
        fields = relax(jnp.pad(fields, ((0, 0), (1, 1), (1, 1))), conduct_pad, sources_pad, solid_pad, 1, 1)
    film_sens = film_gradient(jnp.pad(fields, ((0, 0), (1, 1), (1, 1))), density)
    film_blocks = film_sens.reshape(N_WIDE, CR // 8, 8, N_NARROW, CC // 16, 16).transpose(0, 3, 1, 4, 2, 5).reshape(NB, 128)
    returned = film_blocks[slot_block]
    scaled = returned / denom
    spread = jnp.einsum('ri,kij->rkj', scaled, filter_tiles, precision=FULL_PRECISION)
    spread = jnp.where(present[:, :, None], spread, 0.0)
    sensitivity = jnp.zeros((NB, 128), jnp.float32).at[safe_cols].add(spread)
    return fields[0], sensitivity
```

```python
import jax
import jax.numpy as jnp
from jax import lax
from jax.experimental import pallas as pl
from jax.experimental.pallas import tpu as pltpu
from jax.sharding import PartitionSpec as P

SWEEPS = 16
COND_FLOOR = 0.01
SQUEEZE_DAMPING = 0.25

SLOTS = 2048
SENT = 1536
BROWS = 16
QS = 17
MAIN = 8 * QS * 16
EXT = MAIN + QS * 32
OWNERS = ("wide", "narrow")


def main_row(a, slot, half):
    return (a * QS + slot) * 16 + half * 8


def rim_row(slot, part):
    return MAIN + slot * 32 + part * 8


def lane_ids(shape=(8, 128)):
    return lax.broadcasted_iota(jnp.int32, shape, 1)


def sub_ids(shape=(8, 128)):
    return lax.broadcasted_iota(jnp.int32, shape, 0)


def roll(x, by, axis):
    by = by % x.shape[axis]
    return x if by == 0 else pltpu.roll(x, by, axis)


def curve_offset(first_block):
    inner = first_block & (SLOTS - 1)
    row, col = inner >> 7, inner & 127
    h = (col >> 4) << 8
    for bit in range(4):
        h = h | (((col >> bit) & 1) << (2 * bit)) | (((row >> bit) & 1) << (2 * bit + 1))
    return SENT - h


def inner_place(brow, group):
    low, third = group >> 1, group & 1
    col = third * 8 + low
    place = 0
    for bit in range(4):
        place |= ((col >> bit) & 1) << (2 * bit)
        place |= ((brow >> bit) & 1) << (2 * bit + 1)
    return place


def swap_stages(vecs):
    lane = lane_ids(vecs[0].shape)
    vecs = list(vecs)
    for vec_bit, weight in ((0, 8), (3, 4), (2, 2), (1, 1)):
        upper = (lane & weight) != 0
        new = list(vecs)
        for i in range(16):
            if i & (1 << vec_bit):
                continue
            j = i | (1 << vec_bit)
            a, b = vecs[i], vecs[j]
            new[i] = jnp.where(upper, roll(b, weight, 1), a)
            new[j] = jnp.where(upper, b, roll(a, -weight, 1))
        vecs = new
    return vecs


def column_of(i):
    return ((i & 1) << 3) | (((i >> 3) & 1) << 2) | (((i >> 2) & 1) << 1) | ((i >> 1) & 1)


def east_west(ctr):
    lane = lane_ids()
    first, last, side = ctr[0], ctr[15], ctr[16]
    side_up, side_down = roll(side, 1, 1), roll(side, -1, 1)
    east15 = jnp.where(lane < 112, roll(first, -16, 1), roll(first, 104, 1))
    east15 = jnp.where(lane < 120, east15, roll(first, 119, 1))
    east15 = jnp.where(lane == 127, side_down, east15)
    west0 = jnp.where(lane >= 16, roll(last, 16, 1), roll(last, 24, 1))
    west0 = jnp.where(lane >= 8, west0, roll(last, 9, 1))
    west0 = jnp.where(lane == 0, side_up, west0)
    east16 = jnp.where(lane == 127, roll(first, -1, 1), side_down)
    west16 = jnp.where(lane == 0, roll(last, 1, 1), side_up)
    east = list(ctr[1:16]) + [east15, east16]
    west = [west0] + list(ctr[0:15]) + [west16]
    return east, west


def split3(x):
    high = x.astype(jnp.bfloat16)
    low = (x - high.astype(jnp.float32)).astype(jnp.bfloat16)
    return high, low


def dot3(x, w_high, w_low):
    high, low = split3(x)
    out = jnp.dot(high, w_high, preferred_element_type=jnp.float32)
    out = out + jnp.dot(low, w_high, preferred_element_type=jnp.float32)
    return out + jnp.dot(high, w_low, preferred_element_type=jnp.float32)


def inverse_denoms(sums):
    sub = sub_ids()
    table = {}
    for kind in range(3):
        base = sums[0]
        if kind != 0:
            base = base + sums[1]
        if kind != 2:
            base = base + sums[2]
        left = jnp.broadcast_to(sums[3], (8, 128))
        right = jnp.broadcast_to(sums[4], (8, 128))
        table[kind, 1] = 1.0 / (base + left + right)
        table[kind, 0] = 1.0 / (base + jnp.where(sub == 0, 0.0, left) + right)
        table[kind, 15] = 1.0 / (base + left + jnp.where(sub == 7, 0.0, right))

    def pick(brow, group):
        kind = 0 if brow == 0 else (2 if brow == BROWS - 1 else 1)
        return table[kind, group if group in (0, 15) else 1]

    return pick


def from_left(vecs, group):
    if group >= 2:
        return vecs(group - 2)
    if group == 1:
        return vecs(14)
    return jnp.where(sub_ids() == 0, 0.0, roll(vecs(15), 1, 0))


def from_right(vecs, group):
    if group < 14:
        return vecs(group + 2)
    if group == 14:
        return vecs(1)
    return jnp.where(sub_ids() == 7, 0.0, roll(vecs(0), -1, 0))


def sources_kernel(ok_ref, sq_ref, fw_ref, holes_ref, below_ref, above_ref, left_ref, right_ref,
                   out_sq, out_fw):
    lane = lane_ids()

    def spread(load, store):
        vecs = swap_stages([load(v) for v in range(16)])
        for i in range(16):
            store(column_of(i), vecs[i])

    def tile_rows(brow, carry):
        rows = pl.ds(pl.multiple_of(brow * 8, 8), 8)

        def masked(v):
            cols = pl.ds(v * 128, 128)
            return jnp.where(holes_ref[rows, cols] > 0, 0.0, fw_ref[rows, cols])

        def put(ref):
            def store(c, x):
                ref[pl.ds(c * 16 + brow, 8, stride=QS * 16), :] = x

            return store

        spread(lambda v: sq_ref[rows, pl.ds(v * 128, 128)], put(out_sq))
        spread(masked, put(out_fw))
        return carry

    lax.fori_loop(0, BROWS, tile_rows, 0)

    for field, out in ((0, out_sq), (1, out_fw)):
        for part in range(4):
            src = below_ref if part < 2 else above_ref
            ok = ok_ref[1] if part < 2 else ok_ref[0]
            rows = pl.ds(field * 16 + (part % 2) * 8, 8)

            def load(v, src=src, rows=rows, ok=ok):
                return jnp.where(ok > 0, src[rows, pl.ds(v * 128, 128)], 0.0)

            def store(c, x, part=part, out=out):
                out[pl.ds(rim_row(c, part), 8), :] = x

            spread(load, store)
        for block in range(20):
            rows = pl.ds(field * 160 + block * 8, 8)
            keep_right = (lane <= 16) & (ok_ref[3] > 0)
            keep_left = (lane >= 111) & (ok_ref[2] > 0)
            side = jnp.where(keep_right, right_ref[rows, :], jnp.where(keep_left, left_ref[rows, :], 0.0))
            if block < 16:
                out[pl.ds(16 * 16 + block, 8, stride=QS * 16), :] = side
            else:
                part = block - 16
                ok = ok_ref[1] if part < 2 else ok_ref[0]
                out[pl.ds(rim_row(16, part), 8), :] = jnp.where(ok > 0, side, 0.0)


def filter_kernel(first_ref, got_ref, own_ref, tiles_ref, dens_ref, up_ref, down_ref, cols_ref,
                  slots, blocks, prod, edge, sems):
    get = pltpu.make_async_copy(got_ref, slots.at[pl.ds(0, SENT)], sems.at[0])
    own = pltpu.make_async_copy(own_ref, slots.at[pl.ds(SENT, SLOTS)], sems.at[1])
    get.start()
    own.start()
    tiles = tiles_ref[...]
    t_high, t_low = split3(tiles)
    sums = [jnp.sum(tiles[:, k * 128:(k + 1) * 128], axis=0, keepdims=True) for k in range(5)]
    inverse = inverse_denoms(sums)
    offset = curve_offset(first_ref[0])
    get.wait()
    own.wait()
    for brow in range(BROWS):
        for group in range(16):
            blocks[pl.ds(brow * 128 + group * 8, 8), :] = slots[
                pl.ds(offset + inner_place(brow, group), 8, stride=256), :
            ]

    def multiply(brow, carry):
        rows = pl.ds(pl.multiple_of(brow * 128, 128), 128)
        prod[rows, :] = dot3(blocks[rows, :], t_high, t_low)
        return carry

    lax.fori_loop(0, BROWS, multiply, 0)

    def part(k, brow):
        return lambda group: prod[pl.ds(brow * 128 + group * 8, 8), pl.ds(k * 128, 128)]

    for brow in range(BROWS):
        vecs = []
        for group in range(16):
            x = part(0, brow)(group)
            if brow > 0:
                x = x + part(1, brow - 1)(group)
            if brow < BROWS - 1:
                x = x + part(2, brow + 1)(group)
            x = x + from_left(part(3, brow), group)
            x = x + from_right(part(4, brow), group)
            vecs.append(x * inverse(brow, group))
        edge[pl.ds(0 * 16 + brow, 1), :] = vecs[0][0:1]
        edge[pl.ds(1 * 16 + brow, 1), :] = vecs[2][0:1]
        edge[pl.ds(2 * 16 + brow, 1), :] = vecs[13][7:8]
        edge[pl.ds(3 * 16 + brow, 1), :] = vecs[15][7:8]
        turned = jnp.concatenate(vecs, axis=0).T
        for a in range(8):
            dens_ref[pl.ds(a * QS * 16 + brow, 16, stride=16), :] = turned[a * 16:(a + 1) * 16]
        if brow == 0:
            up_ref[0:128, :] = turned
        if brow == 1:
            up_ref[128:256, :] = turned
        if brow == 2:
            up_ref[256:272, :] = turned[0:16]
        if brow == 13:
            down_ref[256:272, :] = turned[112:128]
        if brow == 14:
            down_ref[0:128, :] = turned
        if brow == 15:
            down_ref[128:256, :] = turned
    lane = lane_ids((16, 128))
    c0, c1, c126, c127 = (edge[pl.ds(i * 16, 16), :] for i in range(4))
    for a in range(8):
        x = jnp.where(lane < 16, roll(c0, -16 * a, 1), 0.0)
        x = jnp.where(lane == 16, roll(c1, 16 - 16 * a, 1), x)
        x = jnp.where(lane == 111, roll(c126, 96 - 16 * a, 1), x)
        x = jnp.where(lane >= 112, roll(c127, 112 - 16 * a, 1), x)
        cols_ref[pl.ds(a * 16, 16), :] = x


def corner_kernel(below_ref, above_ref, cols_ref, out_ref):
    out_ref[0:128, :] = cols_ref[...]
    lane = lane_ids()
    sub = sub_ids()
    for part in range(5):
        if part < 4:
            src = below_ref if part < 2 else above_ref

            def load(c, src=src, part=part):
                return src[pl.ds(c + (part % 2) * 128, 8, stride=16), :]
        else:

            def load(c):
                low = jnp.broadcast_to(below_ref[pl.ds(256 + c, 1), :], (8, 128))
                high = jnp.broadcast_to(above_ref[pl.ds(256 + c, 1), :], (8, 128))
                return jnp.where(sub == 0, low, high)

        x = jnp.zeros((8, 128), jnp.float32)
        for c in range(16):
            here = load(c)
            x = jnp.where(lane == c, roll(here, c, 1), x)
            x = jnp.where(lane == 112 + c, roll(here, c - 15, 1), x)
            if c == 0:
                x = jnp.where(lane == 16, here, x)
            if c == 15:
                x = jnp.where(lane == 111, here, x)
        out_ref[pl.ds(128 + part * 8, 8), :] = x


def solve_kernel(ok_ref, first_ref, dens_ref, below_ref, above_ref, left_ref, right_ref, sq_ref, fw_ref,
                 tiles_ref, p_out, back_ref, keep_ref,
                 k, far, wn, ws, we, ww, bp, ba, pp, aa, blocks, prod, slots, sems):
    lane = lane_ids()
    sub = sub_ids()
    up_ok, down_ok, left_ok, right_ok = (ok_ref[i] > 0 for i in range(4))

    def conduct(d):
        return COND_FLOOR + (1.0 - COND_FLOOR) * d * d * d

    def fill(a, carry):
        for slot in range(16):
            for half in range(2):
                rows = pl.ds(pl.multiple_of((a * QS + slot) * 16 + half * 8, 8), 8)
                k[rows, :] = conduct(dens_ref[rows, :])
        return carry

    lax.fori_loop(0, 8, fill, 0)
    keep_right = (lane <= 16) & right_ok
    keep_left = (lane >= 111) & left_ok

    def side(rows):
        d = jnp.where(lane < 64, right_ref[rows, :], left_ref[rows, :])
        return jnp.where(keep_right | keep_left, conduct(d), 0.0)

    for a in range(8):
        for half in range(2):
            k[pl.ds(main_row(a, 16, half), 8), :] = side(pl.ds(a * 16 + half * 8, 8))
    for part in range(4):
        src, ok = (below_ref, down_ok) if part < 2 else (above_ref, up_ok)
        for slot in range(16):
            d = src[pl.ds(slot + (part % 2) * 128, 8, stride=16), :]
            k[pl.ds(rim_row(slot, part), 8), :] = jnp.where(ok, conduct(d), 0.0)
        k[pl.ds(rim_row(16, part), 8), :] = jnp.where(ok, side(pl.ds(128 + part * 8, 8)), 0.0)
    keep_far = ((sub == 0) & down_ok) | ((sub == 7) & up_ok)
    for slot in range(16):
        low = jnp.broadcast_to(below_ref[pl.ds(256 + slot, 1), :], (8, 128))
        high = jnp.broadcast_to(above_ref[pl.ds(256 + slot, 1), :], (8, 128))
        d = jnp.where(sub == 0, low, high)
        far[pl.ds(slot * 8, 8), :] = jnp.where(keep_far, conduct(d), 0.0)
    far[pl.ds(128, 8), :] = jnp.where(keep_far, side(pl.ds(160, 8)), 0.0)

    def vec(ref, base, row):
        if isinstance(base, int) and isinstance(row, int):
            return ref[pl.ds(base + row, 8), :]
        return ref[pl.ds(pl.multiple_of(base + row, 8), 8), :]

    def down_by_one(above, here):
        return jnp.where(sub == 0, roll(above, 1, 0), roll(here, 1, 0))

    def up_by_one(below, here):
        return jnp.where(sub == 7, roll(below, -1, 0), roll(here, -1, 0))

    def group(ref, base, a, half):
        ctr = [vec(ref, base, main_row(a, s, half)) for s in range(QS)]
        north, south = [], []
        for s in range(QS):
            if isinstance(a, int) and a == 0:
                if half == 0:
                    north.append(down_by_one(vec(ref, base, rim_row(s, 3)), vec(ref, base, main_row(7, s, 0))))
                else:
                    north.append(down_by_one(vec(ref, base, main_row(7, s, 0)), vec(ref, base, main_row(7, s, 1))))
            else:
                north.append(vec(ref, base, main_row(a - 1, s, half)))
            if isinstance(a, int) and a == 7:
                if half == 0:
                    south.append(up_by_one(vec(ref, base, main_row(0, s, 1)), vec(ref, base, main_row(0, s, 0))))
                else:
                    south.append(up_by_one(vec(ref, base, rim_row(s, 0)), vec(ref, base, main_row(0, s, 1))))
            else:
                south.append(vec(ref, base, main_row(a + 1, s, half)))
        return ctr, north, south

    def rim_group(ref, base, part, outer=None):
        ctr = [vec(ref, base, rim_row(s, part)) for s in range(QS)]
        north, south = [], []
        for s in range(QS):
            if part == 0:
                above = vec(ref, base, main_row(7, s, 1))
            elif part == 2:
                above = ctr[s] if outer is None else outer[pl.ds(s * 8, 8), :]
            else:
                above = vec(ref, base, rim_row(s, part - 1))
            if part == 3:
                below = vec(ref, base, main_row(0, s, 0))
            elif part == 1:
                below = ctr[s] if outer is None else outer[pl.ds(s * 8, 8), :]
            else:
                below = vec(ref, base, rim_row(s, part + 1))
            north.append(down_by_one(above, ctr[s]))
            south.append(up_by_one(below, ctr[s]))
        return ctr, north, south

    def each_group(body, parts):
        def inner(a, carry):
            for half in range(2):
                body(a, half, None)
            return carry

        lax.fori_loop(1, 7, inner, 0)
        for a in (0, 7):
            for half in range(2):
                body(a, half, None)
        for part in parts:
            body(None, None, part)

    def row_of(a, half, part, s):
        if part is not None:
            return rim_row(s, part)
        return main_row(a, s, half)

    def coefficients(a, half, part):
        ctr, north, south = group(k, 0, a, half) if part is None else rim_group(k, 0, part, far)
        east, west = east_west(ctr)
        for s in range(QS):
            row = row_of(a, half, part, s)
            rows = pl.ds(row if isinstance(row, int) else pl.multiple_of(row, 8), 8)
            fn, fs, fe, fv = (0.5 * (ctr[s] + other[s]) for other in (north, south, east, west))
            weight = fw_ref[rows, :]
            inv = jnp.where(weight > 0.0, 1.0, 0.0) / (fn + fs + fv + fe + SQUEEZE_DAMPING)
            wn[rows, :] = fn * inv
            ws[rows, :] = fs * inv
            we[rows, :] = fe * inv
            ww[rows, :] = fv * inv
            first_p = sq_ref[rows, :] * inv
            first_a = weight * inv
            bp[rows, :] = first_p
            ba[rows, :] = first_a
            pp[rows, :] = first_p
            aa[rows, :] = first_a

    each_group(coefficients, range(4))

    def sweep(src, dst, parts):
        def body(a, half, part):
            for ref, start in ((pp, bp), (aa, ba)):
                ctr, north, south = group(ref, src, a, half) if part is None else rim_group(ref, src, part)
                east, west = east_west(ctr)
                for s in range(QS):
                    row = row_of(a, half, part, s)
                    x = vec(start, 0, row) + vec(wn, 0, row) * north[s]
                    x = x + vec(ws, 0, row) * south[s]
                    x = x + vec(we, 0, row) * east[s]
                    x = x + vec(ww, 0, row) * west[s]
                    ref[pl.ds(pl.multiple_of(dst + row, 8), 8), :] = x

        each_group(body, parts)

    def one(parts):
        def step(i, carry):
            src = lax.rem(i, 2) * EXT
            sweep(src, EXT - src, parts)
            return carry

        return step

    half_way = SWEEPS // 2
    lax.fori_loop(0, half_way - 1, one(range(4)), 0)
    lax.fori_loop(half_way - 1, SWEEPS - 1, one((0, 3)), 0)
    last = ((SWEEPS - 1) % 2) * EXT

    def gradient(a, half, part):
        p_c, p_n, p_s = group(pp, last, a, half)
        p_e, p_w = east_west(p_c)
        a_c, a_n, a_s = group(aa, last, a, half)
        a_e, a_w = east_west(a_c)
        for s in range(16):
            row = main_row(a, s, half)
            total = (a_c[s] - a_n[s]) * (p_c[s] - p_n[s])
            total = total + (a_c[s] - a_s[s]) * (p_c[s] - p_s[s])
            total = total + (a_c[s] - a_w[s]) * (p_c[s] - p_w[s])
            total = total + (a_c[s] - a_e[s]) * (p_c[s] - p_e[s])
            d = vec(dens_ref, 0, row)
            rows = pl.ds(row if isinstance(row, int) else pl.multiple_of(row, 8), 8)
            k[rows, :] = -0.5 * total * (3.0 * (1.0 - COND_FLOOR)) * d * d
            p_out[rows, :] = p_c[s]

    each_group(gradient, ())

    tiles = tiles_ref[...]
    t_high, t_low = split3(tiles[:, :640])
    sums = [jnp.sum(tiles[:, 640 + i * 128:640 + (i + 1) * 128], axis=0, keepdims=True) for i in range(5)]
    inverse = inverse_denoms(sums)
    for brow in range(BROWS):
        film = jnp.concatenate(
            [k[pl.ds(a * QS * 16 + brow, 16, stride=16), :] for a in range(8)], axis=0
        ).T
        for g in range(16):
            blocks[pl.ds(brow * 128 + g * 8, 8), :] = film[g * 8:(g + 1) * 8] * inverse(brow, g)

    def multiply(brow, carry):
        rows = pl.ds(pl.multiple_of(brow * 128, 128), 128)
        prod[rows, :] = dot3(blocks[rows, :], t_high, t_low)
        return carry

    lax.fori_loop(0, BROWS, multiply, 0)

    def piece(i, brow):
        return lambda g: prod[pl.ds(brow * 128 + g * 8, 8), pl.ds(i * 128, 128)]

    offset = curve_offset(first_ref[0])
    for brow in range(BROWS):
        for g in range(16):
            x = piece(0, brow)(g)
            if brow < BROWS - 1:
                x = x + piece(1, brow + 1)(g)
            if brow > 0:
                x = x + piece(2, brow - 1)(g)
            x = x + from_right(piece(3, brow), g)
            x = x + from_left(piece(4, brow), g)
            slots[pl.ds(offset + inner_place(brow, g), 8, stride=256), :] = x
    back = pltpu.make_async_copy(slots.at[pl.ds(0, SENT)], back_ref, sems.at[0])
    keep = pltpu.make_async_copy(slots.at[pl.ds(SENT, SLOTS)], keep_ref, sems.at[1])
    back.start()
    keep.start()
    back.wait()
    keep.wait()


def pressure_kernel(p_ref, out_ref):
    order = [column_of(i) for i in range(16)]

    def tile_rows(brow, carry):
        vecs = [p_ref[pl.ds(c * 16 + brow, 8, stride=QS * 16), :] for c in order]
        vecs = swap_stages(vecs)
        rows = pl.ds(pl.multiple_of(brow * 8, 8), 8)
        for v in range(16):
            out_ref[rows, pl.ds(v * 128, 128)] = vecs[v]
        return carry

    lax.fori_loop(0, BROWS, tile_rows, 0)


def moved(x, axis, by):
    length = lax.axis_size(axis)
    return lax.ppermute(x, axis, [(i, (i + by) % length) for i in range(length)])


def f32(*shape):
    return jax.ShapeDtypeStruct(shape, jnp.float32)


def local(design, filter_tiles, filter_cols, slot_block, holes, squeeze_source, force_weight):
    smem = pl.BlockSpec(memory_space=pltpu.SMEM)
    vmem = pl.BlockSpec(memory_space=pltpu.VMEM)
    hbm = pl.BlockSpec(memory_space=pl.ANY)
    params = pltpu.CompilerParams(vmem_limit_bytes=56 * 1024 * 1024)
    wide, narrow = lax.axis_index("wide"), lax.axis_index("narrow")
    inside = jnp.stack([
        wide > 0, wide < lax.axis_size("wide") - 1, narrow > 0, narrow < lax.axis_size("narrow") - 1,
    ]).astype(jnp.int32)
    first = slot_block[0:1]
    taps = filter_tiles.transpose(2, 0, 1).reshape(128, 640)
    back_taps = jnp.concatenate([filter_tiles.transpose(1, 0, 2).reshape(128, 640), taps], axis=1)

    got = moved(design[SLOTS - SENT:], OWNERS, 1)

    def edge_rows(rows):
        weight = jnp.where(holes[rows] > 0, 0.0, force_weight[rows])
        return jnp.concatenate([squeeze_source[rows], weight], axis=0)

    below = moved(edge_rows(slice(0, 16)), "wide", -1)
    above = moved(edge_rows(slice(112, 128)), "wide", 1)

    def ends(x):
        lane = lax.broadcasted_iota(jnp.int32, (1, 128), 1)
        return jnp.where(lane < 64, x[:, :128], x[:, -128:])

    masked = jnp.where(ends(holes) > 0, 0.0, ends(force_weight))
    sides = jnp.concatenate([
        ends(squeeze_source), ends(below[:16]), ends(above[:16]),
        masked, ends(below[16:]), ends(above[16:]),
    ], axis=0)
    right = moved(sides, "narrow", -1)
    left = moved(sides, "narrow", 1)
    sq, fw = pl.pallas_call(
        sources_kernel,
        out_shape=(f32(EXT, 128), f32(EXT, 128)),
        in_specs=[smem] + [vmem] * 7,
        compiler_params=params,
        name="sources",
    )(inside, squeeze_source, force_weight, holes, below, above, left, right)

    dens, up, down, cols = pl.pallas_call(
        filter_kernel,
        out_shape=(f32(MAIN, 128), f32(272, 128), f32(272, 128), f32(128, 128)),
        in_specs=[smem, hbm, hbm, vmem],
        scratch_shapes=[
            pltpu.VMEM((SENT + SLOTS, 128), jnp.float32),
            pltpu.VMEM((SLOTS, 128), jnp.float32),
            pltpu.VMEM((SLOTS, 640), jnp.float32),
            pltpu.VMEM((64, 128), jnp.float32),
            pltpu.SemaphoreType.DMA((2,)),
        ],
        compiler_params=params,
        name="filter",
    )(first, got, design, taps)
    d_below = moved(up, "wide", -1)
    d_above = moved(down, "wide", 1)
    d_sides = pl.pallas_call(
        corner_kernel, out_shape=f32(168, 128), compiler_params=params, name="corners",
    )(d_below, d_above, cols)
    d_right = moved(d_sides, "narrow", -1)
    d_left = moved(d_sides, "narrow", 1)

    big = pltpu.VMEM((EXT, 128), jnp.float32)
    twice = pltpu.VMEM((2 * EXT, 128), jnp.float32)
    p_film, back, keep = pl.pallas_call(
        solve_kernel,
        out_shape=(f32(MAIN, 128), f32(SENT, 128), f32(SLOTS, 128)),
        in_specs=[smem, smem] + [vmem] * 8,
        out_specs=(vmem, hbm, hbm),
        scratch_shapes=[
            big, pltpu.VMEM((QS * 8, 128), jnp.float32), big, big, big, big, big, big, twice, twice,
            pltpu.VMEM((SLOTS, 128), jnp.float32),
            pltpu.VMEM((SLOTS, 640), jnp.float32),
            pltpu.VMEM((SENT + SLOTS, 128), jnp.float32),
            pltpu.SemaphoreType.DMA((2,)),
        ],
        compiler_params=params,
        name="solve",
    )(inside, first, dens, d_below, d_above, d_left, d_right, sq, fw, back_taps)
    returned = moved(back, OWNERS, -1)
    pressure = pl.pallas_call(
        pressure_kernel, out_shape=f32(128, 2048), compiler_params=params, name="pressure",
    )(p_film)
    held = curve_offset(first[0]) + (SLOTS - SENT)
    slot = lax.broadcasted_iota(jnp.int32, (SLOTS, 1), 0)
    tail = jnp.pad(returned, ((SLOTS - SENT, 0), (0, 0)))
    sensitivity = jnp.where(slot < held, keep, tail)
    return pressure, sensitivity


def solution(mesh):
    placed = (
        P(OWNERS, None),
        P(),
        P(OWNERS, None),
        P(OWNERS),
        P("wide", "narrow"),
        P("wide", "narrow"),
        P("wide", "narrow"),
    )
    return jax.shard_map(
        local,
        mesh=mesh,
        in_specs=placed,
        out_specs=(P("wide", "narrow"), P(OWNERS, None)),
        check_vma=False,
    )
```

```python
import jax
import jax.numpy as jnp
from jax import lax
from jax.experimental import pallas as pl
from jax.experimental.pallas import tpu as pltpu
from jax.sharding import PartitionSpec as P

SWEEPS = 16
CHUNK = 3
UNROLL = False
MROWS = 512
ROOM = (10, 16, 4, 34, 4, 4)
COND_FLOOR = 0.01
SQUEEZE_DAMPING = 0.25

SLOTS = 2048
SENT = 1536
BROWS = 16
QS = 17
MAIN = 8 * QS * 16
RIMS = QS * 32
EXT = MAIN + RIMS
OWNERS = ("wide", "narrow")


def main_row(a, slot, half):
    return (a * QS + slot) * 16 + half * 8


def rim_row(slot, part):
    return MAIN + slot * 32 + part * 8


def lane_ids(shape=(8, 128)):
    return lax.broadcasted_iota(jnp.int32, shape, 1)


def sub_ids(shape=(8, 128)):
    return lax.broadcasted_iota(jnp.int32, shape, 0)


def roll(x, by, axis):
    by = by % x.shape[axis]
    return x if by == 0 else pltpu.roll(x, by, axis)


def curve_offset(first_block):
    inner = first_block & (SLOTS - 1)
    row, col = inner >> 7, inner & 127
    h = (col >> 4) << 8
    for bit in range(4):
        h = h | (((col >> bit) & 1) << (2 * bit)) | (((row >> bit) & 1) << (2 * bit + 1))
    return SENT - h


def inner_place(brow, group):
    low, third = group >> 1, group & 1
    col = third * 8 + low
    place = 0
    for bit in range(4):
        place |= ((col >> bit) & 1) << (2 * bit)
        place |= ((brow >> bit) & 1) << (2 * bit + 1)
    return place


def swap_stages(vecs):
    lane = lane_ids(vecs[0].shape)
    vecs = list(vecs)
    for vec_bit, weight in ((0, 8), (3, 4), (2, 2), (1, 1)):
        upper = (lane & weight) != 0
        new = list(vecs)
        for i in range(16):
            if i & (1 << vec_bit):
                continue
            j = i | (1 << vec_bit)
            a, b = vecs[i], vecs[j]
            new[i] = jnp.where(upper, roll(b, weight, 1), a)
            new[j] = jnp.where(upper, b, roll(a, -weight, 1))
        vecs = new
    return vecs


def column_of(i):
    return ((i & 1) << 3) | (((i >> 3) & 1) << 2) | (((i >> 2) & 1) << 1) | ((i >> 1) & 1)


def east_west(ctr):
    lane = lane_ids()
    first, last, side = ctr[0], ctr[15], ctr[16]
    side_up, side_down = roll(side, 1, 1), roll(side, -1, 1)
    east15 = jnp.where(lane < 112, roll(first, -16, 1), roll(first, 104, 1))
    east15 = jnp.where(lane < 120, east15, roll(first, 119, 1))
    east15 = jnp.where(lane == 127, side_down, east15)
    west0 = jnp.where(lane >= 16, roll(last, 16, 1), roll(last, 24, 1))
    west0 = jnp.where(lane >= 8, west0, roll(last, 9, 1))
    west0 = jnp.where(lane == 0, side_up, west0)
    east16 = jnp.where(lane == 127, roll(first, -1, 1), side_down)
    west16 = jnp.where(lane == 0, roll(last, 1, 1), side_up)
    east = list(ctr[1:16]) + [east15, east16]
    west = [west0] + list(ctr[0:15]) + [west16]
    return east, west


def split(x):
    high = x.astype(jnp.bfloat16)
    low = (x - high.astype(jnp.float32)).astype(jnp.bfloat16)
    return high, low


def stacked(w):
    high, low = split(w)
    return jnp.concatenate([high, high, low], axis=0)


def put_parts(parts, rows, x):
    high, low = split(x)
    parts[rows, 0:128] = high
    parts[rows, 128:256] = low
    parts[rows, 256:384] = high


def inverse_denoms(sums):
    sub = sub_ids()
    table = {}
    for kind in range(3):
        base = sums[0]
        if kind != 0:
            base = base + sums[1]
        if kind != 2:
            base = base + sums[2]
        left = jnp.broadcast_to(sums[3], (8, 128))
        right = jnp.broadcast_to(sums[4], (8, 128))
        table[kind, 1] = 1.0 / (base + left + right)
        table[kind, 0] = 1.0 / (base + jnp.where(sub == 0, 0.0, left) + right)
        table[kind, 15] = 1.0 / (base + left + jnp.where(sub == 7, 0.0, right))

    def pick(brow, group):
        kind = 0 if brow == 0 else (2 if brow == BROWS - 1 else 1)
        return table[kind, group if group in (0, 15) else 1]

    return pick


def from_left(vecs, group):
    if group >= 2:
        return vecs(group - 2)
    if group == 1:
        return vecs(14)
    return jnp.where(sub_ids() == 0, 0.0, roll(vecs(15), 1, 0))


def from_right(vecs, group):
    if group < 14:
        return vecs(group + 2)
    if group == 14:
        return vecs(1)
    return jnp.where(sub_ids() == 7, 0.0, roll(vecs(0), -1, 0))


def spread(load, store):
    vecs = swap_stages([load(v) for v in range(16)])
    for i in range(16):
        store(column_of(i), vecs[i])


def sources_kernel(sq_ref, fw_ref, holes_ref, out_sq, out_fw):
    def tile_rows(brow, carry):
        rows = pl.ds(pl.multiple_of(brow * 8, 8), 8)

        def masked(v):
            cols = pl.ds(v * 128, 128)
            return jnp.where(holes_ref[rows, cols] > 0, 0.0, fw_ref[rows, cols])

        def put(ref):
            def store(c, x):
                ref[pl.ds(c * 16 + brow, 8, stride=256), :] = x

            return store

        spread(lambda v: sq_ref[rows, pl.ds(v * 128, 128)], put(out_sq))
        spread(masked, put(out_fw))
        return carry

    lax.fori_loop(0, BROWS, tile_rows, 0, unroll=2)


def rims_kernel(ok_ref, below_ref, above_ref, left_ref, right_ref, out_sq, out_fw):
    lane = lane_ids()
    keep_right = (lane <= 16) & (ok_ref[3] > 0)
    keep_left = (lane >= 111) & (ok_ref[2] > 0)
    for field, out in ((0, out_sq), (1, out_fw)):
        for part in range(4):
            src = below_ref if part < 2 else above_ref
            ok = ok_ref[1] if part < 2 else ok_ref[0]
            rows = pl.ds(field * 16 + (part % 2) * 8, 8)

            def load(v, src=src, rows=rows, ok=ok):
                return jnp.where(ok > 0, src[rows, pl.ds(v * 128, 128)], 0.0)

            def store(c, x, part=part, out=out):
                out[pl.ds(c * 32 + part * 8, 8), :] = x

            spread(load, store)
        for block in range(20):
            rows = pl.ds(field * 160 + block * 8, 8)
            side = jnp.where(keep_right, right_ref[rows, :], jnp.where(keep_left, left_ref[rows, :], 0.0))
            if block < 16:
                out[pl.ds(RIMS + block, 8, stride=16), :] = side
            else:
                part = block - 16
                ok = ok_ref[1] if part < 2 else ok_ref[0]
                out[pl.ds(16 * 32 + part * 8, 8), :] = jnp.where(ok > 0, side, 0.0)


def filter_kernel(first_ref, got_ref, own_ref, tiles_ref, dens_ref, up_ref, down_ref, cols_ref,
                  slots, parts, prod, edge):
    tiles = [tiles_ref[i].T for i in range(5)]
    inverse = inverse_denoms([jnp.sum(t, axis=0, keepdims=True) for t in tiles])
    weights = stacked(jnp.concatenate(tiles, axis=1))
    offset = curve_offset(first_ref[0])
    slots[pl.ds(0, SENT), :] = got_ref[...]
    slots[pl.ds(SENT, SLOTS), :] = own_ref[...]
    for brow in range(BROWS):
        x = jnp.concatenate(
            [slots[pl.ds(offset + inner_place(brow, g), 8, stride=256), :] for g in range(16)], axis=0
        )
        put_parts(parts, pl.ds(brow * 128, 128), x)
    for i in range(SLOTS // MROWS):
        rows = pl.ds(i * MROWS, MROWS)
        prod[rows, :] = jnp.dot(parts[rows, :], weights, preferred_element_type=jnp.float32)

    def part(k, brow):
        return lambda group: prod[pl.ds(brow * 128 + group * 8, 8), pl.ds(k * 128, 128)]

    for brow in range(BROWS):
        vecs = []
        for group in range(16):
            x = part(0, brow)(group)
            if brow > 0:
                x = x + part(1, brow - 1)(group)
            if brow < BROWS - 1:
                x = x + part(2, brow + 1)(group)
            x = x + from_left(part(3, brow), group)
            x = x + from_right(part(4, brow), group)
            vecs.append(x * inverse(brow, group))
        edge[pl.ds(0 * 16 + brow, 1), :] = vecs[0][0:1]
        edge[pl.ds(1 * 16 + brow, 1), :] = vecs[2][0:1]
        edge[pl.ds(2 * 16 + brow, 1), :] = vecs[13][7:8]
        edge[pl.ds(3 * 16 + brow, 1), :] = vecs[15][7:8]
        turned = jnp.concatenate(vecs, axis=0).T
        for a in range(8):
            dens_ref[pl.ds(a * QS * 16 + brow, 16, stride=16), :] = turned[a * 16:(a + 1) * 16]
        if brow == 0:
            up_ref[0:128, :] = turned
        if brow == 1:
            up_ref[128:256, :] = turned
        if brow == 2:
            up_ref[256:272, :] = turned[0:16]
        if brow == 13:
            down_ref[256:272, :] = turned[112:128]
        if brow == 14:
            down_ref[0:128, :] = turned
        if brow == 15:
            down_ref[128:256, :] = turned
    lane = lane_ids((16, 128))
    c0, c1, c126, c127 = (edge[pl.ds(i * 16, 16), :] for i in range(4))
    for a in range(8):
        x = jnp.where(lane < 16, roll(c0, -16 * a, 1), 0.0)
        x = jnp.where(lane == 16, roll(c1, 16 - 16 * a, 1), x)
        x = jnp.where(lane == 111, roll(c126, 96 - 16 * a, 1), x)
        x = jnp.where(lane >= 112, roll(c127, 112 - 16 * a, 1), x)
        cols_ref[pl.ds(a * 16, 16), :] = x


def corner_kernel(below_ref, above_ref, cols_ref, out_ref):
    out_ref[0:128, :] = cols_ref[...]
    lane = lane_ids()
    sub = sub_ids()
    for part in range(5):
        if part < 4:
            src = below_ref if part < 2 else above_ref

            def load(c, src=src, part=part):
                return src[pl.ds(c + (part % 2) * 128, 8, stride=16), :]
        else:

            def load(c):
                low = jnp.broadcast_to(below_ref[pl.ds(256 + c, 1), :], (8, 128))
                high = jnp.broadcast_to(above_ref[pl.ds(256 + c, 1), :], (8, 128))
                return jnp.where(sub == 0, low, high)

        x = jnp.zeros((8, 128), jnp.float32)
        for c in range(16):
            here = load(c)
            x = jnp.where(lane == c, roll(here, c, 1), x)
            x = jnp.where(lane == 112 + c, roll(here, c - 15, 1), x)
            if c == 0:
                x = jnp.where(lane == 16, here, x)
            if c == 15:
                x = jnp.where(lane == 111, here, x)
        out_ref[pl.ds(128 + part * 8, 8), :] = x


def solve_kernel(ok_ref, first_ref, dens_ref, below_ref, above_ref, left_ref, right_ref, sq_ref, fw_ref,
                 sq_rim, fw_rim, tiles_ref, p_out, back_ref, keep_ref,
                 k, far, wn, ws, we, ww, bp, ba, p0, p1, a0, a1, parts, prod, slots):
    lane = lane_ids()
    sub = sub_ids()
    up_ok, down_ok, left_ok, right_ok = (ok_ref[i] > 0 for i in range(4))

    def conduct(d):
        return COND_FLOOR + (1.0 - COND_FLOOR) * d * d * d

    def fill(a, carry):
        for slot in range(16):
            for half in range(2):
                rows = pl.ds(pl.multiple_of((a * QS + slot) * 16 + half * 8, 8), 8)
                k[rows, :] = conduct(dens_ref[rows, :])
        return carry

    lax.fori_loop(0, 8, fill, 0)
    keep_right = (lane <= 16) & right_ok
    keep_left = (lane >= 111) & left_ok

    def side(rows):
        d = jnp.where(lane < 64, right_ref[rows, :], left_ref[rows, :])
        return jnp.where(keep_right | keep_left, conduct(d), 0.0)

    for a in range(8):
        for half in range(2):
            k[pl.ds(main_row(a, 16, half), 8), :] = side(pl.ds(a * 16 + half * 8, 8))
    for part in range(4):
        src, ok = (below_ref, down_ok) if part < 2 else (above_ref, up_ok)
        for slot in range(16):
            d = src[pl.ds(slot + (part % 2) * 128, 8, stride=16), :]
            k[pl.ds(rim_row(slot, part), 8), :] = jnp.where(ok, conduct(d), 0.0)
        k[pl.ds(rim_row(16, part), 8), :] = jnp.where(ok, side(pl.ds(128 + part * 8, 8)), 0.0)
    keep_far = ((sub == 0) & down_ok) | ((sub == 7) & up_ok)
    for slot in range(16):
        low = jnp.broadcast_to(below_ref[pl.ds(256 + slot, 1), :], (8, 128))
        high = jnp.broadcast_to(above_ref[pl.ds(256 + slot, 1), :], (8, 128))
        d = jnp.where(sub == 0, low, high)
        far[pl.ds(slot * 8, 8), :] = jnp.where(keep_far, conduct(d), 0.0)
    far[pl.ds(128, 8), :] = jnp.where(keep_far, side(pl.ds(160, 8)), 0.0)

    def vec(ref, base, row):
        if isinstance(base, int) and isinstance(row, int):
            return ref[pl.ds(base + row, 8), :]
        return ref[pl.ds(pl.multiple_of(base + row, 8), 8), :]

    def rows_at(row):
        return pl.ds(row if isinstance(row, int) else pl.multiple_of(row, 8), 8)

    def down_by_one(above, here):
        return jnp.where(sub == 0, roll(above, 1, 0), roll(here, 1, 0))

    def up_by_one(below, here):
        return jnp.where(sub == 7, roll(below, -1, 0), roll(here, -1, 0))

    def group(ref, base, a, half):
        ctr = [vec(ref, base, main_row(a, s, half)) for s in range(QS)]
        north, south = [], []
        for s in range(QS):
            if isinstance(a, int) and a == 0:
                if half == 0:
                    north.append(down_by_one(vec(ref, base, rim_row(s, 3)), vec(ref, base, main_row(7, s, 0))))
                else:
                    north.append(down_by_one(vec(ref, base, main_row(7, s, 0)), vec(ref, base, main_row(7, s, 1))))
            else:
                north.append(vec(ref, base, main_row(a - 1, s, half)))
            if isinstance(a, int) and a == 7:
                if half == 0:
                    south.append(up_by_one(vec(ref, base, main_row(0, s, 1)), vec(ref, base, main_row(0, s, 0))))
                else:
                    south.append(up_by_one(vec(ref, base, rim_row(s, 0)), vec(ref, base, main_row(0, s, 1))))
            else:
                south.append(vec(ref, base, main_row(a + 1, s, half)))
        return ctr, north, south

    def rim_group(ref, base, part, outer=None):
        ctr = [vec(ref, base, rim_row(s, part)) for s in range(QS)]
        north, south = [], []
        for s in range(QS):
            if part == 0:
                above = vec(ref, base, main_row(7, s, 1))
            elif part == 2:
                above = ctr[s] if outer is None else outer[pl.ds(s * 8, 8), :]
            else:
                above = vec(ref, base, rim_row(s, part - 1))
            if part == 3:
                below = vec(ref, base, main_row(0, s, 0))
            elif part == 1:
                below = ctr[s] if outer is None else outer[pl.ds(s * 8, 8), :]
            else:
                below = vec(ref, base, rim_row(s, part + 1))
            north.append(down_by_one(above, ctr[s]))
            south.append(up_by_one(below, ctr[s]))
        return ctr, north, south

    def each_group(body, parts):
        def inner(a, carry):
            for half in range(2):
                body(a, half, None)
            return carry

        lax.fori_loop(1, 7, inner, 0)
        for a in (0, 7):
            for half in range(2):
                body(a, half, None)
        for part in parts:
            body(None, None, part)

    def row_of(a, half, part, s):
        if part is not None:
            return rim_row(s, part)
        return main_row(a, s, half)

    def coefficients(a, half, part):
        ctr, north, south = group(k, 0, a, half) if part is None else rim_group(k, 0, part, far)
        east, west = east_west(ctr)
        for s in range(QS):
            row = row_of(a, half, part, s)
            rows = pl.ds(row if isinstance(row, int) else pl.multiple_of(row, 8), 8)
            if part is not None:
                source, sources = pl.ds(s * 32 + part * 8, 8), (sq_rim, fw_rim)
            elif s == 16:
                source, sources = rows_at(RIMS + a * 16 + half * 8), (sq_rim, fw_rim)
            else:
                source, sources = rows_at((a * 16 + s) * 16 + half * 8), (sq_ref, fw_ref)
            fn, fs, fe, fv = (0.5 * (ctr[s] + other[s]) for other in (north, south, east, west))
            weight = sources[1][source, :]
            inv = jnp.where(weight > 0.0, 1.0, 0.0) / (fn + fs + fv + fe + SQUEEZE_DAMPING)
            wn[rows, :] = fn * inv
            ws[rows, :] = fs * inv
            we[rows, :] = fe * inv
            ww[rows, :] = fv * inv
            first_p = sources[0][source, :] * inv
            first_a = weight * inv
            bp[rows, :] = first_p
            ba[rows, :] = first_a
            p0[rows, :] = first_p
            a0[rows, :] = first_a

    each_group(coefficients, range(4))

    def ends_of(ref, row):
        first, last, beside = (vec(ref, 0, row(s)) for s in (0, 15, 16))
        east, west = east_west([first] + [None] * 14 + [last, beside])
        return {15: east[15], 16: east[16]}, {0: west[0], 16: west[16]}

    def sweep(old, new, full):
        def relax(rows, neighbours):
            ends = [[ends_of(ref, row) for row in rows] for ref in old]
            before = [[None] * len(rows) for _ in old]
            here = [[vec(ref, 0, row(0)) for row in rows] for ref in old]
            for s in range(QS):
                after = [[vec(ref, 0, row(s + 1)) if s < QS - 1 else None for row in rows] for ref in old]
                around = [neighbours(f, s, here[f]) for f in range(2)]
                for i, row in enumerate(rows):
                    at = row(s)
                    cn, cs, ce, cw = (vec(c, 0, at) for c in (wn, ws, we, ww))
                    for f, start in enumerate((bp, ba)):
                        north, south = around[f][i]
                        east = ends[f][i][0].get(s, after[f][i])
                        west = ends[f][i][1].get(s, before[f][i])
                        x = (vec(start, 0, at) + cn * north) + (cs * south + (ce * east + cw * west))
                        new[f][rows_at(at), :] = x
                before, here = here, after

        def chunk(i, carry):
            a = CHUNK * i + 1
            for half in range(2):
                def neighbours(f, s, ctr, half=half):
                    north = vec(old[f], 0, main_row(a - 1, s, half))
                    south = vec(old[f], 0, main_row(a + CHUNK, s, half))
                    column = [north] + ctr + [south]
                    return [(column[j], column[j + 2]) for j in range(CHUNK)]

                relax([lambda s, half=half, j=j: main_row(a + j, s, half) for j in range(CHUNK)], neighbours)
            return carry

        if UNROLL:
            for i in range(6 // CHUNK):
                chunk(i, 0)
        else:
            lax.fori_loop(0, 6 // CHUNK, chunk, 0)

        ring = [
            lambda s: main_row(7, s, 0), lambda s: main_row(7, s, 1),
            lambda s: main_row(0, s, 0), lambda s: main_row(0, s, 1),
            lambda s: rim_row(s, 0), lambda s: rim_row(s, 3),
        ]
        if full:
            ring += [lambda s: rim_row(s, 1), lambda s: rim_row(s, 2)]

        def ring_neighbours(f, s, ctr):
            down = [roll(x, 1, 0) for x in ctr]
            up = [roll(x, -1, 0) for x in ctr]
            top, low = sub == 0, sub == 7
            ref = old[f]
            out = [
                (vec(ref, 0, main_row(6, s, 0)), jnp.where(low, up[3], up[2])),
                (vec(ref, 0, main_row(6, s, 1)), jnp.where(low, up[4], up[3])),
                (jnp.where(top, down[5], down[0]), vec(ref, 0, main_row(1, s, 0))),
                (jnp.where(top, down[0], down[1]), vec(ref, 0, main_row(1, s, 1))),
                (jnp.where(top, down[1], down[4]), jnp.where(low, up[6], up[4]) if full else up[4]),
                (jnp.where(top, down[7], down[5]) if full else down[5], jnp.where(low, up[2], up[5])),
            ]
            if full:
                out += [(jnp.where(top, down[4], down[6]), up[6]), (down[7], jnp.where(low, up[5], up[7]))]
            return out

        relax(ring, ring_neighbours)

    def two_sweeps(full):
        def step(i, carry):
            sweep((p0, a0), (p1, a1), full)
            sweep((p1, a1), (p0, a0), full)
            return carry

        return step

    lax.fori_loop(0, 4, two_sweeps(True), 0)
    lax.fori_loop(0, 3, two_sweeps(False), 0)
    sweep((p0, a0), (p1, a1), False)
    last = 0

    def gradient(a, half, part):
        p_c, p_n, p_s = group(p1, last, a, half)
        p_e, p_w = east_west(p_c)
        a_c, a_n, a_s = group(a1, last, a, half)
        a_e, a_w = east_west(a_c)
        for s in range(16):
            row = main_row(a, s, half)
            total = (a_c[s] - a_n[s]) * (p_c[s] - p_n[s])
            total = total + (a_c[s] - a_s[s]) * (p_c[s] - p_s[s])
            total = total + (a_c[s] - a_w[s]) * (p_c[s] - p_w[s])
            total = total + (a_c[s] - a_e[s]) * (p_c[s] - p_e[s])
            d = vec(dens_ref, 0, row)
            rows = pl.ds(row if isinstance(row, int) else pl.multiple_of(row, 8), 8)
            k[rows, :] = -0.5 * total * (3.0 * (1.0 - COND_FLOOR)) * d * d
            p_out[rows, :] = p_c[s]

    each_group(gradient, ())

    inverse = inverse_denoms([jnp.sum(tiles_ref[i].T, axis=0, keepdims=True) for i in range(5)])
    weights = stacked(jnp.concatenate([tiles_ref[i] for i in range(5)], axis=1))
    for brow in range(BROWS):
        film = jnp.concatenate(
            [k[pl.ds(a * QS * 16 + brow, 16, stride=16), :] for a in range(8)], axis=0
        ).T
        film = jnp.concatenate([film[g * 8:(g + 1) * 8] * inverse(brow, g) for g in range(16)], axis=0)
        put_parts(parts, pl.ds(brow * 128, 128), film)
    for i in range(SLOTS // MROWS):
        rows = pl.ds(i * MROWS, MROWS)
        prod[rows, :] = jnp.dot(parts[rows, :], weights, preferred_element_type=jnp.float32)

    def piece(i, brow):
        return lambda g: prod[pl.ds(brow * 128 + g * 8, 8), pl.ds(i * 128, 128)]

    offset = curve_offset(first_ref[0])
    for brow in range(BROWS):
        for g in range(16):
            x = piece(0, brow)(g)
            if brow < BROWS - 1:
                x = x + piece(1, brow + 1)(g)
            if brow > 0:
                x = x + piece(2, brow - 1)(g)
            x = x + from_right(piece(3, brow), g)
            x = x + from_left(piece(4, brow), g)
            slots[pl.ds(offset + inner_place(brow, g), 8, stride=256), :] = x
    back_ref[...] = slots[pl.ds(0, SENT), :]
    keep_ref[...] = slots[pl.ds(SENT, SLOTS), :]


def pressure_kernel(p_ref, out_ref):
    order = [column_of(i) for i in range(16)]

    def tile_rows(brow, carry):
        vecs = [p_ref[pl.ds(c * 16 + brow, 8, stride=QS * 16), :] for c in order]
        vecs = swap_stages(vecs)
        rows = pl.ds(pl.multiple_of(brow * 8, 8), 8)
        for v in range(16):
            out_ref[rows, pl.ds(v * 128, 128)] = vecs[v]
        return carry

    lax.fori_loop(0, BROWS, tile_rows, 0, unroll=4)


def moved(x, axis, by):
    length = lax.axis_size(axis)
    return lax.ppermute(x, axis, [(i, (i + by) % length) for i in range(length)])


def room(mib):
    return pltpu.CompilerParams(vmem_limit_bytes=mib * 1024 * 1024)


def work(flops, moved_bytes):
    return pl.CostEstimate(flops=flops, transcendentals=0, bytes_accessed=moved_bytes)


def f32(*shape):
    return jax.ShapeDtypeStruct(shape, jnp.float32)


def local(design, filter_tiles, filter_cols, slot_block, holes, squeeze_source, force_weight):
    smem = pl.BlockSpec(memory_space=pltpu.SMEM)
    vmem = pl.BlockSpec(memory_space=pltpu.VMEM)
    wide, narrow = lax.axis_index("wide"), lax.axis_index("narrow")
    inside = jnp.stack([
        wide > 0, wide < lax.axis_size("wide") - 1, narrow > 0, narrow < lax.axis_size("narrow") - 1,
    ]).astype(jnp.int32)
    first = slot_block[0:1]
    tail, holes, squeeze_source, force_weight = lax.optimization_barrier(
        (design[SLOTS - SENT:], holes, squeeze_source, force_weight)
    )
    got = moved(tail, OWNERS, 1)
    sq, fw = pl.pallas_call(
        sources_kernel,
        out_shape=(f32(SLOTS, 128), f32(SLOTS, 128)),
        compiler_params=room(ROOM[0]),
        cost_estimate=work(2000000, 5000000),
        name="sources",
    )(squeeze_source, force_weight, holes)
    sq, fw, first, holes, squeeze_source, force_weight = lax.optimization_barrier(
        (sq, fw, first, holes, squeeze_source, force_weight)
    )

    def edge_rows(rows):
        weight = jnp.where(holes[rows] > 0, 0.0, force_weight[rows])
        return jnp.concatenate([squeeze_source[rows], weight], axis=0)

    below = moved(edge_rows(slice(0, 16)), "wide", -1)
    above = moved(edge_rows(slice(112, 128)), "wide", 1)

    def ends(x):
        lane = lax.broadcasted_iota(jnp.int32, (1, 128), 1)
        return jnp.where(lane < 64, x[:, :128], x[:, -128:])

    masked = jnp.where(ends(holes) > 0, 0.0, ends(force_weight))
    sides = jnp.concatenate([
        ends(squeeze_source), ends(below[:16]), ends(above[:16]),
        masked, ends(below[16:]), ends(above[16:]),
    ], axis=0)
    right = moved(sides, "narrow", -1)
    left = moved(sides, "narrow", 1)
    sq_rim, fw_rim = pl.pallas_call(
        rims_kernel,
        out_shape=(f32(RIMS + 128, 128), f32(RIMS + 128, 128)),
        in_specs=[smem] + [vmem] * 4,
        compiler_params=room(ROOM[5]),
        cost_estimate=work(500000, 1200000),
        name="rims",
    )(inside, below, above, left, right)

    dens, up, down, cols = pl.pallas_call(
        filter_kernel,
        out_shape=(f32(MAIN, 128), f32(272, 128), f32(272, 128), f32(128, 128)),
        in_specs=[smem, vmem, vmem, vmem],
        scratch_shapes=[
            pltpu.VMEM((SENT + SLOTS, 128), jnp.float32),
            pltpu.VMEM((SLOTS, 384), jnp.bfloat16),
            pltpu.VMEM((SLOTS, 640), jnp.float32),
            pltpu.VMEM((64, 128), jnp.float32),
        ],
        compiler_params=room(ROOM[1]),
        cost_estimate=work(1100000000, 3500000),
        name="filter",
    )(first, got, design, filter_tiles)
    d_below = moved(up, "wide", -1)
    d_above = moved(down, "wide", 1)
    d_sides = pl.pallas_call(
        corner_kernel, out_shape=f32(168, 128), compiler_params=room(ROOM[2]), cost_estimate=work(200000, 500000), name="corners",
    )(d_below, d_above, cols)
    d_right = moved(d_sides, "narrow", -1)
    d_left = moved(d_sides, "narrow", 1)

    big = pltpu.VMEM((EXT, 128), jnp.float32)
    p_film, back, keep = pl.pallas_call(
        solve_kernel,
        out_shape=(f32(MAIN, 128), f32(SENT, 128), f32(SLOTS, 128)),
        in_specs=[smem, smem] + [vmem] * 10,
        scratch_shapes=[
            big, pltpu.VMEM((QS * 8, 128), jnp.float32), big, big, big, big, big, big, big, big, big, big,
            pltpu.VMEM((SLOTS, 384), jnp.bfloat16),
            pltpu.VMEM((SLOTS, 640), jnp.float32),
            pltpu.VMEM((SENT + SLOTS, 128), jnp.float32),
        ],
        compiler_params=room(ROOM[3]),
        cost_estimate=work(1400000000, 9000000),
        name="solve",
    )(inside, first, dens, d_below, d_above, d_left, d_right, sq, fw, sq_rim, fw_rim, filter_tiles)
    returned = moved(back, OWNERS, -1)
    pressure = pl.pallas_call(
        pressure_kernel, out_shape=f32(128, 2048), compiler_params=room(ROOM[4]), cost_estimate=work(2000000, 2100000), name="pressure",
    )(p_film)
    held = curve_offset(first[0]) + (SLOTS - SENT)
    slot = lax.broadcasted_iota(jnp.int32, (SLOTS, 1), 0)
    upper = jnp.pad(returned, ((SLOTS - SENT, 0), (0, 0)))
    sensitivity = jnp.where(slot < held, keep, upper)
    return pressure, sensitivity


def solution(mesh):
    placed = (
        P(OWNERS, None),
        P(),
        P(OWNERS, None),
        P(OWNERS),
        P("wide", "narrow"),
        P("wide", "narrow"),
        P("wide", "narrow"),
    )
    return jax.shard_map(
        local,
        mesh=mesh,
        in_specs=placed,
        out_specs=(P("wide", "narrow"), P(OWNERS, None)),
        check_vma=False,
    )
```

```python
import jax
import jax.numpy as jnp
from jax import lax
from jax.experimental import pallas as pl
from jax.experimental.pallas import tpu as pltpu
from jax.sharding import PartitionSpec as P

SWEEPS = 16
CHUNK = 3
UNROLL = False
MROWS = 512
ROOM = (10, 11, 4, 30, 4, 4)
COND_FLOOR = 0.01
SQUEEZE_DAMPING = 0.25

SLOTS = 2048
SENT = 1536
BROWS = 16
QS = 17
MAIN = 8 * QS * 16
RIMS = QS * 32
EXT = MAIN + RIMS
OWNERS = ("wide", "narrow")


def main_row(a, slot, half):
    return (a * QS + slot) * 16 + half * 8


def rim_row(slot, part):
    return MAIN + slot * 32 + part * 8


def lane_ids(shape=(8, 128)):
    return lax.broadcasted_iota(jnp.int32, shape, 1)


def sub_ids(shape=(8, 128)):
    return lax.broadcasted_iota(jnp.int32, shape, 0)


def roll(x, by, axis):
    by = by % x.shape[axis]
    return x if by == 0 else pltpu.roll(x, by, axis)


def curve_offset(first_block):
    inner = first_block & (SLOTS - 1)
    row, col = inner >> 7, inner & 127
    h = (col >> 4) << 8
    for bit in range(4):
        h = h | (((col >> bit) & 1) << (2 * bit)) | (((row >> bit) & 1) << (2 * bit + 1))
    return SENT - h


def inner_place(brow, group):
    low, third = group >> 1, group & 1
    col = third * 8 + low
    place = 0
    for bit in range(4):
        place |= ((col >> bit) & 1) << (2 * bit)
        place |= ((brow >> bit) & 1) << (2 * bit + 1)
    return place


def swap_stages(vecs):
    lane = lane_ids(vecs[0].shape)
    vecs = list(vecs)
    for vec_bit, weight in ((0, 8), (3, 4), (2, 2), (1, 1)):
        upper = (lane & weight) != 0
        new = list(vecs)
        for i in range(16):
            if i & (1 << vec_bit):
                continue
            j = i | (1 << vec_bit)
            a, b = vecs[i], vecs[j]
            new[i] = jnp.where(upper, roll(b, weight, 1), a)
            new[j] = jnp.where(upper, b, roll(a, -weight, 1))
        vecs = new
    return vecs


def column_of(i):
    return ((i & 1) << 3) | (((i >> 3) & 1) << 2) | (((i >> 2) & 1) << 1) | ((i >> 1) & 1)


def east_west(ctr):
    lane = lane_ids()
    first, last, side = ctr[0], ctr[15], ctr[16]
    side_up, side_down = roll(side, 1, 1), roll(side, -1, 1)
    east15 = jnp.where(lane < 112, roll(first, -16, 1), roll(first, 104, 1))
    east15 = jnp.where(lane < 120, east15, roll(first, 119, 1))
    east15 = jnp.where(lane == 127, side_down, east15)
    west0 = jnp.where(lane >= 16, roll(last, 16, 1), roll(last, 24, 1))
    west0 = jnp.where(lane >= 8, west0, roll(last, 9, 1))
    west0 = jnp.where(lane == 0, side_up, west0)
    east16 = jnp.where(lane == 127, roll(first, -1, 1), side_down)
    west16 = jnp.where(lane == 0, roll(last, 1, 1), side_up)
    east = list(ctr[1:16]) + [east15, east16]
    west = [west0] + list(ctr[0:15]) + [west16]
    return east, west


def split(x):
    high = x.astype(jnp.bfloat16)
    low = (x - high.astype(jnp.float32)).astype(jnp.bfloat16)
    return high, low


def stacked(w):
    high, low = split(w)
    return jnp.concatenate([high, high, low], axis=0)


def put_parts(parts, rows, x):
    high, low = split(x)
    parts[rows, 0:128] = high
    parts[rows, 128:256] = low
    parts[rows, 256:384] = high


def inverse_denoms(sums):
    sub = sub_ids()
    table = {}
    for kind in range(3):
        base = sums[0]
        if kind != 0:
            base = base + sums[1]
        if kind != 2:
            base = base + sums[2]
        left = jnp.broadcast_to(sums[3], (8, 128))
        right = jnp.broadcast_to(sums[4], (8, 128))
        table[kind, 1] = 1.0 / (base + left + right)
        table[kind, 0] = 1.0 / (base + jnp.where(sub == 0, 0.0, left) + right)
        table[kind, 15] = 1.0 / (base + left + jnp.where(sub == 7, 0.0, right))

    def pick(brow, group):
        kind = 0 if brow == 0 else (2 if brow == BROWS - 1 else 1)
        return table[kind, group if group in (0, 15) else 1]

    return pick


def from_left(vecs, group):
    if group >= 2:
        return vecs(group - 2)
    if group == 1:
        return vecs(14)
    return jnp.where(sub_ids() == 0, 0.0, roll(vecs(15), 1, 0))


def from_right(vecs, group):
    if group < 14:
        return vecs(group + 2)
    if group == 14:
        return vecs(1)
    return jnp.where(sub_ids() == 7, 0.0, roll(vecs(0), -1, 0))


def spread(load, store):
    vecs = swap_stages([load(v) for v in range(16)])
    for i in range(16):
        store(column_of(i), vecs[i])


def outer_columns(ref, rows):
    return jnp.where(lane_ids() < 64, ref[rows, 0:128], ref[rows, 1920:2048])


def sources_kernel(sq_ref, fw_ref, holes_ref, out_sq, out_fw, sides, edge_up, edge_down):
    for edge, start in ((edge_up, 0), (edge_down, 112)):
        for part in range(2):
            rows = pl.ds(start + part * 8, 8)
            edge[pl.ds(part * 8, 8), :] = sq_ref[rows, :]
            edge[pl.ds(16 + part * 8, 8), :] = jnp.where(holes_ref[rows, :] > 0, 0.0, fw_ref[rows, :])
    for brow in range(BROWS):
        rows = pl.ds(brow * 8, 8)
        sides[rows, :] = outer_columns(sq_ref, rows)
        outer = jnp.where(outer_columns(holes_ref, rows) > 0, 0.0, outer_columns(fw_ref, rows))
        sides[pl.ds(128 + brow * 8, 8), :] = outer

    def tile_rows(brow, carry):
        rows = pl.ds(pl.multiple_of(brow * 8, 8), 8)

        def masked(v):
            cols = pl.ds(v * 128, 128)
            return jnp.where(holes_ref[rows, cols] > 0, 0.0, fw_ref[rows, cols])

        def put(ref):
            def store(c, x):
                ref[pl.ds(c * 16 + brow, 8, stride=256), :] = x

            return store

        spread(lambda v: sq_ref[rows, pl.ds(v * 128, 128)], put(out_sq))
        spread(masked, put(out_fw))
        return carry

    lax.fori_loop(0, BROWS, tile_rows, 0, unroll=2)


def rims_kernel(ok_ref, below_ref, above_ref, sides_ref, out_sq, out_fw, out_sides):
    for field, out in ((0, out_sq), (1, out_fw)):
        for part in range(4):
            src = below_ref if part < 2 else above_ref
            ok = ok_ref[1] if part < 2 else ok_ref[0]
            rows = pl.ds(field * 16 + (part % 2) * 8, 8)

            def load(v, src=src, rows=rows, ok=ok):
                return jnp.where(ok > 0, src[rows, pl.ds(v * 128, 128)], 0.0)

            def store(c, x, part=part, out=out):
                out[pl.ds(c * 32 + part * 8, 8), :] = x

            spread(load, store)
            outer = jnp.where(ok > 0, outer_columns(src, rows), 0.0)
            out_sides[pl.ds(field * 160 + 128 + part * 8, 8), :] = outer
        out_sides[pl.ds(field * 160, 128), :] = sides_ref[pl.ds(field * 128, 128), :]


def filter_kernel(first_ref, got_ref, own_ref, tiles_ref, dens_ref, up_ref, down_ref, cols_ref,
                  slots, parts, prod, edge):
    tiles = [tiles_ref[i].T for i in range(5)]
    inverse = inverse_denoms([jnp.sum(t, axis=0, keepdims=True) for t in tiles])
    weights = stacked(jnp.concatenate(tiles, axis=1))
    offset = curve_offset(first_ref[0])
    slots[pl.ds(0, SENT), :] = got_ref[...]
    slots[pl.ds(SENT, SLOTS), :] = own_ref[...]
    for brow in range(BROWS):
        x = jnp.concatenate(
            [slots[pl.ds(offset + inner_place(brow, g), 8, stride=256), :] for g in range(16)], axis=0
        )
        put_parts(parts, pl.ds(brow * 128, 128), x)
    for i in range(SLOTS // MROWS):
        rows = pl.ds(i * MROWS, MROWS)
        prod[rows, :] = jnp.dot(parts[rows, :], weights, preferred_element_type=jnp.float32)

    def part(k, brow):
        return lambda group: prod[pl.ds(brow * 128 + group * 8, 8), pl.ds(k * 128, 128)]

    for brow in range(BROWS):
        vecs = []
        for group in range(16):
            x = part(0, brow)(group)
            if brow > 0:
                x = x + part(1, brow - 1)(group)
            if brow < BROWS - 1:
                x = x + part(2, brow + 1)(group)
            x = x + from_left(part(3, brow), group)
            x = x + from_right(part(4, brow), group)
            vecs.append(x * inverse(brow, group))
        edge[pl.ds(0 * 16 + brow, 1), :] = vecs[0][0:1]
        edge[pl.ds(1 * 16 + brow, 1), :] = vecs[2][0:1]
        edge[pl.ds(2 * 16 + brow, 1), :] = vecs[13][7:8]
        edge[pl.ds(3 * 16 + brow, 1), :] = vecs[15][7:8]
        turned = jnp.concatenate(vecs, axis=0).T
        for a in range(8):
            dens_ref[pl.ds(a * QS * 16 + brow, 16, stride=16), :] = turned[a * 16:(a + 1) * 16]
        if brow == 0:
            up_ref[0:128, :] = turned
        if brow == 1:
            up_ref[128:256, :] = turned
        if brow == 2:
            up_ref[256:272, :] = turned[0:16]
        if brow == 13:
            down_ref[256:272, :] = turned[112:128]
        if brow == 14:
            down_ref[0:128, :] = turned
        if brow == 15:
            down_ref[128:256, :] = turned
    lane = lane_ids((16, 128))
    c0, c1, c126, c127 = (edge[pl.ds(i * 16, 16), :] for i in range(4))
    for a in range(8):
        x = jnp.where(lane < 16, roll(c0, -16 * a, 1), 0.0)
        x = jnp.where(lane == 16, roll(c1, 16 - 16 * a, 1), x)
        x = jnp.where(lane == 111, roll(c126, 96 - 16 * a, 1), x)
        x = jnp.where(lane >= 112, roll(c127, 112 - 16 * a, 1), x)
        cols_ref[pl.ds(a * 16, 16), :] = x


def corner_kernel(below_ref, above_ref, cols_ref, sides_ref, out_ref):
    out_ref[0:128, :] = cols_ref[...]
    out_ref[168:488, :] = sides_ref[...]
    lane = lane_ids()
    sub = sub_ids()
    for part in range(5):
        if part < 4:
            src = below_ref if part < 2 else above_ref

            def load(c, src=src, part=part):
                return src[pl.ds(c + (part % 2) * 128, 8, stride=16), :]
        else:

            def load(c):
                low = jnp.broadcast_to(below_ref[pl.ds(256 + c, 1), :], (8, 128))
                high = jnp.broadcast_to(above_ref[pl.ds(256 + c, 1), :], (8, 128))
                return jnp.where(sub == 0, low, high)

        x = jnp.zeros((8, 128), jnp.float32)
        for c in range(16):
            here = load(c)
            x = jnp.where(lane == c, roll(here, c, 1), x)
            x = jnp.where(lane == 112 + c, roll(here, c - 15, 1), x)
            if c == 0:
                x = jnp.where(lane == 16, here, x)
            if c == 15:
                x = jnp.where(lane == 111, here, x)
        out_ref[pl.ds(128 + part * 8, 8), :] = x


def solve_kernel(ok_ref, first_ref, dens_ref, below_ref, above_ref, left_ref, right_ref, sq_ref, fw_ref,
                 sq_rim, fw_rim, tiles_ref, p_out, back_ref, keep_ref,
                 k, far, wn, ws, we, ww, bp, ba, p0, p1, a0, a1, parts, prod, slots):
    lane = lane_ids()
    sub = sub_ids()
    up_ok, down_ok, left_ok, right_ok = (ok_ref[i] > 0 for i in range(4))

    def conduct(d):
        return COND_FLOOR + (1.0 - COND_FLOOR) * d * d * d

    def fill(a, carry):
        for slot in range(16):
            for half in range(2):
                rows = pl.ds(pl.multiple_of((a * QS + slot) * 16 + half * 8, 8), 8)
                k[rows, :] = conduct(dens_ref[rows, :])
        return carry

    lax.fori_loop(0, 8, fill, 0)
    keep_right = (lane <= 16) & right_ok
    keep_left = (lane >= 111) & left_ok

    def side(rows):
        d = jnp.where(lane < 64, right_ref[rows, :], left_ref[rows, :])
        return jnp.where(keep_right | keep_left, conduct(d), 0.0)

    for a in range(8):
        for half in range(2):
            k[pl.ds(main_row(a, 16, half), 8), :] = side(pl.ds(a * 16 + half * 8, 8))
    for part in range(4):
        src, ok = (below_ref, down_ok) if part < 2 else (above_ref, up_ok)
        for slot in range(16):
            d = src[pl.ds(slot + (part % 2) * 128, 8, stride=16), :]
            k[pl.ds(rim_row(slot, part), 8), :] = jnp.where(ok, conduct(d), 0.0)
        k[pl.ds(rim_row(16, part), 8), :] = jnp.where(ok, side(pl.ds(128 + part * 8, 8)), 0.0)
    keep_far = ((sub == 0) & down_ok) | ((sub == 7) & up_ok)
    for slot in range(16):
        low = jnp.broadcast_to(below_ref[pl.ds(256 + slot, 1), :], (8, 128))
        high = jnp.broadcast_to(above_ref[pl.ds(256 + slot, 1), :], (8, 128))
        d = jnp.where(sub == 0, low, high)
        far[pl.ds(slot * 8, 8), :] = jnp.where(keep_far, conduct(d), 0.0)
    far[pl.ds(128, 8), :] = jnp.where(keep_far, side(pl.ds(160, 8)), 0.0)

    def vec(ref, base, row):
        if isinstance(base, int) and isinstance(row, int):
            return ref[pl.ds(base + row, 8), :]
        return ref[pl.ds(pl.multiple_of(base + row, 8), 8), :]

    def rows_at(row):
        return pl.ds(row if isinstance(row, int) else pl.multiple_of(row, 8), 8)

    def down_by_one(above, here):
        return jnp.where(sub == 0, roll(above, 1, 0), roll(here, 1, 0))

    def up_by_one(below, here):
        return jnp.where(sub == 7, roll(below, -1, 0), roll(here, -1, 0))

    def group(ref, base, a, half):
        ctr = [vec(ref, base, main_row(a, s, half)) for s in range(QS)]
        north, south = [], []
        for s in range(QS):
            if isinstance(a, int) and a == 0:
                if half == 0:
                    north.append(down_by_one(vec(ref, base, rim_row(s, 3)), vec(ref, base, main_row(7, s, 0))))
                else:
                    north.append(down_by_one(vec(ref, base, main_row(7, s, 0)), vec(ref, base, main_row(7, s, 1))))
            else:
                north.append(vec(ref, base, main_row(a - 1, s, half)))
            if isinstance(a, int) and a == 7:
                if half == 0:
                    south.append(up_by_one(vec(ref, base, main_row(0, s, 1)), vec(ref, base, main_row(0, s, 0))))
                else:
                    south.append(up_by_one(vec(ref, base, rim_row(s, 0)), vec(ref, base, main_row(0, s, 1))))
            else:
                south.append(vec(ref, base, main_row(a + 1, s, half)))
        return ctr, north, south

    def rim_group(ref, base, part, outer=None):
        ctr = [vec(ref, base, rim_row(s, part)) for s in range(QS)]
        north, south = [], []
        for s in range(QS):
            if part == 0:
                above = vec(ref, base, main_row(7, s, 1))
            elif part == 2:
                above = ctr[s] if outer is None else outer[pl.ds(s * 8, 8), :]
            else:
                above = vec(ref, base, rim_row(s, part - 1))
            if part == 3:
                below = vec(ref, base, main_row(0, s, 0))
            elif part == 1:
                below = ctr[s] if outer is None else outer[pl.ds(s * 8, 8), :]
            else:
                below = vec(ref, base, rim_row(s, part + 1))
            north.append(down_by_one(above, ctr[s]))
            south.append(up_by_one(below, ctr[s]))
        return ctr, north, south

    def each_group(body, parts):
        def inner(a, carry):
            for half in range(2):
                body(a, half, None)
            return carry

        lax.fori_loop(1, 7, inner, 0)
        for a in (0, 7):
            for half in range(2):
                body(a, half, None)
        for part in parts:
            body(None, None, part)

    def row_of(a, half, part, s):
        if part is not None:
            return rim_row(s, part)
        return main_row(a, s, half)

    def side_sources(a, half, part):
        for field in range(2):
            if part is None:
                rows = pl.ds(168 + field * 160 + half * 64 + a, 8, stride=8)
                ok = True
            else:
                rows = pl.ds(168 + field * 160 + 128 + part * 8, 8)
                ok = down_ok if part < 2 else up_ok
            x = jnp.where(lane < 64, right_ref[rows, :], left_ref[rows, :])
            yield jnp.where((keep_right | keep_left) & ok, x, 0.0)

    def coefficients(a, half, part):
        ctr, north, south = group(k, 0, a, half) if part is None else rim_group(k, 0, part, far)
        east, west = east_west(ctr)
        for s in range(QS):
            row = row_of(a, half, part, s)
            rows = pl.ds(row if isinstance(row, int) else pl.multiple_of(row, 8), 8)
            if s == 16:
                source, weight = side_sources(a, half, part)
            elif part is not None:
                here = pl.ds(s * 32 + part * 8, 8)
                source, weight = sq_rim[here, :], fw_rim[here, :]
            else:
                here = rows_at((a * 16 + s) * 16 + half * 8)
                source, weight = sq_ref[here, :], fw_ref[here, :]
            fn, fs, fe, fv = (0.5 * (ctr[s] + other[s]) for other in (north, south, east, west))
            inv = jnp.where(weight > 0.0, 1.0, 0.0) / (fn + fs + fv + fe + SQUEEZE_DAMPING)
            wn[rows, :] = fn * inv
            ws[rows, :] = fs * inv
            we[rows, :] = fe * inv
            ww[rows, :] = fv * inv
            first_p = source * inv
            first_a = weight * inv
            bp[rows, :] = first_p
            ba[rows, :] = first_a
            p0[rows, :] = first_p
            a0[rows, :] = first_a

    each_group(coefficients, range(4))

    def ends_of(ref, row):
        first, last, beside = (vec(ref, 0, row(s)) for s in (0, 15, 16))
        east, west = east_west([first] + [None] * 14 + [last, beside])
        return {15: east[15], 16: east[16]}, {0: west[0], 16: west[16]}

    def sweep(old, new, full):
        def relax(rows, neighbours):
            ends = [[ends_of(ref, row) for row in rows] for ref in old]
            before = [[None] * len(rows) for _ in old]
            here = [[vec(ref, 0, row(0)) for row in rows] for ref in old]
            for s in range(QS):
                after = [[vec(ref, 0, row(s + 1)) if s < QS - 1 else None for row in rows] for ref in old]
                around = [neighbours(f, s, here[f]) for f in range(2)]
                for i, row in enumerate(rows):
                    at = row(s)
                    cn, cs, ce, cw = (vec(c, 0, at) for c in (wn, ws, we, ww))
                    for f, start in enumerate((bp, ba)):
                        north, south = around[f][i]
                        east = ends[f][i][0].get(s, after[f][i])
                        west = ends[f][i][1].get(s, before[f][i])
                        x = (vec(start, 0, at) + cn * north) + (cs * south + (ce * east + cw * west))
                        new[f][rows_at(at), :] = x
                before, here = here, after

        def chunk(i, carry):
            a = CHUNK * i + 1
            for half in range(2):
                def neighbours(f, s, ctr, half=half):
                    north = vec(old[f], 0, main_row(a - 1, s, half))
                    south = vec(old[f], 0, main_row(a + CHUNK, s, half))
                    column = [north] + ctr + [south]
                    return [(column[j], column[j + 2]) for j in range(CHUNK)]

                relax([lambda s, half=half, j=j: main_row(a + j, s, half) for j in range(CHUNK)], neighbours)
            return carry

        if UNROLL:
            for i in range(6 // CHUNK):
                chunk(i, 0)
        else:
            lax.fori_loop(0, 6 // CHUNK, chunk, 0)

        ring = [
            lambda s: main_row(7, s, 0), lambda s: main_row(7, s, 1),
            lambda s: main_row(0, s, 0), lambda s: main_row(0, s, 1),
            lambda s: rim_row(s, 0), lambda s: rim_row(s, 3),
        ]
        if full:
            ring += [lambda s: rim_row(s, 1), lambda s: rim_row(s, 2)]

        def ring_neighbours(f, s, ctr):
            down = [roll(x, 1, 0) for x in ctr]
            up = [roll(x, -1, 0) for x in ctr]
            top, low = sub == 0, sub == 7
            ref = old[f]
            out = [
                (vec(ref, 0, main_row(6, s, 0)), jnp.where(low, up[3], up[2])),
                (vec(ref, 0, main_row(6, s, 1)), jnp.where(low, up[4], up[3])),
                (jnp.where(top, down[5], down[0]), vec(ref, 0, main_row(1, s, 0))),
                (jnp.where(top, down[0], down[1]), vec(ref, 0, main_row(1, s, 1))),
                (jnp.where(top, down[1], down[4]), jnp.where(low, up[6], up[4]) if full else up[4]),
                (jnp.where(top, down[7], down[5]) if full else down[5], jnp.where(low, up[2], up[5])),
            ]
            if full:
                out += [(jnp.where(top, down[4], down[6]), up[6]), (down[7], jnp.where(low, up[5], up[7]))]
            return out

        relax(ring, ring_neighbours)

    def two_sweeps(full):
        def step(i, carry):
            sweep((p0, a0), (p1, a1), full)
            sweep((p1, a1), (p0, a0), full)
            return carry

        return step

    lax.fori_loop(0, 4, two_sweeps(True), 0)
    lax.fori_loop(0, 3, two_sweeps(False), 0)
    sweep((p0, a0), (p1, a1), False)
    last = 0

    def gradient(a, half, part):
        p_c, p_n, p_s = group(p1, last, a, half)
        p_e, p_w = east_west(p_c)
        a_c, a_n, a_s = group(a1, last, a, half)
        a_e, a_w = east_west(a_c)
        for s in range(16):
            row = main_row(a, s, half)
            total = (a_c[s] - a_n[s]) * (p_c[s] - p_n[s])
            total = total + (a_c[s] - a_s[s]) * (p_c[s] - p_s[s])
            total = total + (a_c[s] - a_w[s]) * (p_c[s] - p_w[s])
            total = total + (a_c[s] - a_e[s]) * (p_c[s] - p_e[s])
            d = vec(dens_ref, 0, row)
            rows = pl.ds(row if isinstance(row, int) else pl.multiple_of(row, 8), 8)
            k[rows, :] = -0.5 * total * (3.0 * (1.0 - COND_FLOOR)) * d * d
            p_out[rows, :] = p_c[s]

    each_group(gradient, ())

    inverse = inverse_denoms([jnp.sum(tiles_ref[i].T, axis=0, keepdims=True) for i in range(5)])
    weights = stacked(jnp.concatenate([tiles_ref[i] for i in range(5)], axis=1))
    for brow in range(BROWS):
        film = jnp.concatenate(
            [k[pl.ds(a * QS * 16 + brow, 16, stride=16), :] for a in range(8)], axis=0
        ).T
        film = jnp.concatenate([film[g * 8:(g + 1) * 8] * inverse(brow, g) for g in range(16)], axis=0)
        put_parts(parts, pl.ds(brow * 128, 128), film)
    for i in range(SLOTS // MROWS):
        rows = pl.ds(i * MROWS, MROWS)
        prod[rows, :] = jnp.dot(parts[rows, :], weights, preferred_element_type=jnp.float32)

    def piece(i, brow):
        return lambda g: prod[pl.ds(brow * 128 + g * 8, 8), pl.ds(i * 128, 128)]

    offset = curve_offset(first_ref[0])
    for brow in range(BROWS):
        for g in range(16):
            x = piece(0, brow)(g)
            if brow < BROWS - 1:
                x = x + piece(1, brow + 1)(g)
            if brow > 0:
                x = x + piece(2, brow - 1)(g)
            x = x + from_right(piece(3, brow), g)
            x = x + from_left(piece(4, brow), g)
            slots[pl.ds(offset + inner_place(brow, g), 8, stride=256), :] = x
    back_ref[...] = slots[pl.ds(0, SENT), :]
    keep_ref[...] = slots[pl.ds(SENT, SLOTS), :]


def pressure_kernel(p_ref, out_ref):
    order = [column_of(i) for i in range(16)]

    def tile_rows(brow, carry):
        vecs = [p_ref[pl.ds(c * 16 + brow, 8, stride=QS * 16), :] for c in order]
        vecs = swap_stages(vecs)
        rows = pl.ds(pl.multiple_of(brow * 8, 8), 8)
        for v in range(16):
            out_ref[rows, pl.ds(v * 128, 128)] = vecs[v]
        return carry

    lax.fori_loop(0, BROWS, tile_rows, 0, unroll=4)


def moved(x, axis, by):
    length = lax.axis_size(axis)
    return lax.ppermute(x, axis, [(i, (i + by) % length) for i in range(length)])


def room(mib):
    return pltpu.CompilerParams(vmem_limit_bytes=mib * 1024 * 1024)


def work(flops, moved_bytes):
    return pl.CostEstimate(flops=flops, transcendentals=0, bytes_accessed=moved_bytes)


def f32(*shape):
    return jax.ShapeDtypeStruct(shape, jnp.float32)


def local(design, filter_tiles, filter_cols, slot_block, holes, squeeze_source, force_weight):
    smem = pl.BlockSpec(memory_space=pltpu.SMEM)
    vmem = pl.BlockSpec(memory_space=pltpu.VMEM)
    wide, narrow = lax.axis_index("wide"), lax.axis_index("narrow")
    inside = jnp.stack([
        wide > 0, wide < lax.axis_size("wide") - 1, narrow > 0, narrow < lax.axis_size("narrow") - 1,
    ]).astype(jnp.int32)
    first = slot_block[0:1]
    tail, holes, squeeze_source, force_weight = lax.optimization_barrier(
        (design[SLOTS - SENT:], holes, squeeze_source, force_weight)
    )
    got = moved(tail, OWNERS, 1)
    sq, fw, sides, edge_up, edge_down = pl.pallas_call(
        sources_kernel,
        out_shape=(f32(SLOTS, 128), f32(SLOTS, 128), f32(256, 128), f32(32, 2048), f32(32, 2048)),
        compiler_params=room(ROOM[0]),
        cost_estimate=work(2000000, 5500000),
        name="sources",
    )(squeeze_source, force_weight, holes)
    below = moved(edge_up, "wide", -1)
    above = moved(edge_down, "wide", 1)

    dens, up, down, cols = pl.pallas_call(
        filter_kernel,
        out_shape=(f32(MAIN, 128), f32(272, 128), f32(272, 128), f32(128, 128)),
        in_specs=[smem, vmem, vmem, vmem],
        scratch_shapes=[
            pltpu.VMEM((SENT + SLOTS, 128), jnp.float32),
            pltpu.VMEM((SLOTS, 384), jnp.bfloat16),
            pltpu.VMEM((SLOTS, 640), jnp.float32),
            pltpu.VMEM((64, 128), jnp.float32),
        ],
        compiler_params=room(ROOM[1]),
        cost_estimate=work(1100000000, 3500000),
        name="filter",
    )(first, got, design, filter_tiles)
    d_below = moved(up, "wide", -1)
    d_above = moved(down, "wide", 1)
    below, above, cols = lax.optimization_barrier((below, above, cols))
    sq_rim, fw_rim, sides = pl.pallas_call(
        rims_kernel,
        out_shape=(f32(512, 128), f32(512, 128), f32(320, 128)),
        in_specs=[smem] + [vmem] * 3,
        compiler_params=room(ROOM[5]),
        cost_estimate=work(500000, 1200000),
        name="rims",
    )(inside, below, above, sides)
    d_sides = pl.pallas_call(
        corner_kernel, out_shape=f32(488, 128), compiler_params=room(ROOM[2]),
        cost_estimate=work(200000, 700000), name="corners",
    )(d_below, d_above, cols, sides)
    d_right = moved(d_sides, "narrow", -1)
    d_left = moved(d_sides, "narrow", 1)

    big = pltpu.VMEM((EXT, 128), jnp.float32)
    p_film, back, keep = pl.pallas_call(
        solve_kernel,
        out_shape=(f32(MAIN, 128), f32(SENT, 128), f32(SLOTS, 128)),
        in_specs=[smem, smem] + [vmem] * 10,
        scratch_shapes=[
            big, pltpu.VMEM((QS * 8, 128), jnp.float32), big, big, big, big, big, big, big, big, big, big,
            pltpu.VMEM((SLOTS, 384), jnp.bfloat16),
            pltpu.VMEM((SLOTS, 640), jnp.float32),
            pltpu.VMEM((SENT + SLOTS, 128), jnp.float32),
        ],
        compiler_params=room(ROOM[3]),
        cost_estimate=work(1400000000, 9000000),
        name="solve",
    )(inside, first, dens, d_below, d_above, d_left, d_right, sq, fw, sq_rim, fw_rim, filter_tiles)
    returned = moved(back, OWNERS, -1)
    pressure = pl.pallas_call(
        pressure_kernel, out_shape=f32(128, 2048), compiler_params=room(ROOM[4]), cost_estimate=work(2000000, 2100000), name="pressure",
    )(p_film)
    held = curve_offset(first[0]) + (SLOTS - SENT)
    slot = lax.broadcasted_iota(jnp.int32, (SLOTS, 1), 0)
    upper = jnp.pad(returned, ((SLOTS - SENT, 0), (0, 0)))
    sensitivity = jnp.where(slot < held, keep, upper)
    return pressure, sensitivity


def solution(mesh):
    placed = (
        P(OWNERS, None),
        P(),
        P(OWNERS, None),
        P(OWNERS),
        P("wide", "narrow"),
        P("wide", "narrow"),
        P("wide", "narrow"),
    )
    return jax.shard_map(
        local,
        mesh=mesh,
        in_specs=placed,
        out_specs=(P("wide", "narrow"), P(OWNERS, None)),
        check_vma=False,
    )
```

```python
import jax
import jax.numpy as jnp
from jax import lax
from jax.experimental import pallas as pl
from jax.experimental.pallas import tpu as pltpu
from jax.sharding import PartitionSpec as P

SWEEPS = 16
CHUNK = 3
UNROLL = False
MROWS = 512
ROOM = (10, 11, 4, 30, 4, 4)
COND_FLOOR = 0.01
SQUEEZE_DAMPING = 0.25

SLOTS = 2048
SENT = 1536
BROWS = 16
QS = 17
MAIN = 8 * QS * 16
RIMS = QS * 32
EXT = MAIN + RIMS
OWNERS = ("wide", "narrow")


def main_row(a, slot, half):
    return (a * QS + slot) * 16 + half * 8


def rim_row(slot, part):
    return MAIN + slot * 32 + part * 8


def lane_ids(shape=(8, 128)):
    return lax.broadcasted_iota(jnp.int32, shape, 1)


def sub_ids(shape=(8, 128)):
    return lax.broadcasted_iota(jnp.int32, shape, 0)


def roll(x, by, axis):
    by = by % x.shape[axis]
    return x if by == 0 else pltpu.roll(x, by, axis)


def curve_offset(first_block):
    inner = first_block & (SLOTS - 1)
    row, col = inner >> 7, inner & 127
    h = (col >> 4) << 8
    for bit in range(4):
        h = h | (((col >> bit) & 1) << (2 * bit)) | (((row >> bit) & 1) << (2 * bit + 1))
    return SENT - h


def inner_place(brow, group):
    low, third = group >> 1, group & 1
    col = third * 8 + low
    place = 0
    for bit in range(4):
        place |= ((col >> bit) & 1) << (2 * bit)
        place |= ((brow >> bit) & 1) << (2 * bit + 1)
    return place


def swap_stages(vecs):
    lane = lane_ids(vecs[0].shape)
    vecs = list(vecs)
    for vec_bit, weight in ((0, 8), (3, 4), (2, 2), (1, 1)):
        upper = (lane & weight) != 0
        new = list(vecs)
        for i in range(16):
            if i & (1 << vec_bit):
                continue
            j = i | (1 << vec_bit)
            a, b = vecs[i], vecs[j]
            new[i] = jnp.where(upper, roll(b, weight, 1), a)
            new[j] = jnp.where(upper, b, roll(a, -weight, 1))
        vecs = new
    return vecs


def column_of(i):
    return ((i & 1) << 3) | (((i >> 3) & 1) << 2) | (((i >> 2) & 1) << 1) | ((i >> 1) & 1)


def east_west(ctr):
    lane = lane_ids()
    first, last, side = ctr[0], ctr[15], ctr[16]
    side_up, side_down = roll(side, 1, 1), roll(side, -1, 1)
    east15 = jnp.where(lane < 112, roll(first, -16, 1), roll(first, 104, 1))
    east15 = jnp.where(lane < 120, east15, roll(first, 119, 1))
    east15 = jnp.where(lane == 127, side_down, east15)
    west0 = jnp.where(lane >= 16, roll(last, 16, 1), roll(last, 24, 1))
    west0 = jnp.where(lane >= 8, west0, roll(last, 9, 1))
    west0 = jnp.where(lane == 0, side_up, west0)
    east16 = jnp.where(lane == 127, roll(first, -1, 1), side_down)
    west16 = jnp.where(lane == 0, roll(last, 1, 1), side_up)
    east = list(ctr[1:16]) + [east15, east16]
    west = [west0] + list(ctr[0:15]) + [west16]
    return east, west


def split(x):
    high = x.astype(jnp.bfloat16)
    low = (x - high.astype(jnp.float32)).astype(jnp.bfloat16)
    return high, low


def stacked(w):
    high, low = split(w)
    return jnp.concatenate([high, high, low], axis=0)


def put_parts(parts, rows, x):
    high, low = split(x)
    parts[rows, 0:128] = high
    parts[rows, 128:256] = low
    parts[rows, 256:384] = high


def inverse_denoms(sums):
    sub = sub_ids()
    table = {}
    for kind in range(3):
        base = sums[0]
        if kind != 0:
            base = base + sums[1]
        if kind != 2:
            base = base + sums[2]
        left = jnp.broadcast_to(sums[3], (8, 128))
        right = jnp.broadcast_to(sums[4], (8, 128))
        table[kind, 1] = 1.0 / (base + left + right)
        table[kind, 0] = 1.0 / (base + jnp.where(sub == 0, 0.0, left) + right)
        table[kind, 15] = 1.0 / (base + left + jnp.where(sub == 7, 0.0, right))

    def pick(brow, group):
        kind = 0 if brow == 0 else (2 if brow == BROWS - 1 else 1)
        return table[kind, group if group in (0, 15) else 1]

    return pick


def from_left(vecs, group):
    if group >= 2:
        return vecs(group - 2)
    if group == 1:
        return vecs(14)
    return jnp.where(sub_ids() == 0, 0.0, roll(vecs(15), 1, 0))


def from_right(vecs, group):
    if group < 14:
        return vecs(group + 2)
    if group == 14:
        return vecs(1)
    return jnp.where(sub_ids() == 7, 0.0, roll(vecs(0), -1, 0))


def spread(load, store):
    vecs = swap_stages([load(v) for v in range(16)])
    for i in range(16):
        store(column_of(i), vecs[i])


def outer_columns(ref, rows):
    return jnp.where(lane_ids() < 64, ref[rows, 0:128], ref[rows, 1920:2048])


def sources_kernel(sq_hbm, fw_hbm, holes_hbm, out_sq, out_fw, sides, edge_up, edge_down,
                   sq_ref, fw_ref, holes_ref, sems):
    copies = []
    for piece in range(4):
        rows = pl.ds(piece * 32, 32)
        copies.append([
            pltpu.make_async_copy(src.at[rows, :], dst.at[rows, :], sems.at[piece, i])
            for i, (src, dst) in enumerate(((sq_hbm, sq_ref), (fw_hbm, fw_ref), (holes_hbm, holes_ref)))
        ])
        for copy in copies[-1]:
            copy.start()

    def tile_rows(brow, carry):
        rows = pl.ds(pl.multiple_of(brow * 8, 8), 8)

        def masked(v):
            cols = pl.ds(v * 128, 128)
            return jnp.where(holes_ref[rows, cols] > 0, 0.0, fw_ref[rows, cols])

        def put(ref):
            def store(c, x):
                ref[pl.ds(c * 16 + brow, 8, stride=256), :] = x

            return store

        spread(lambda v: sq_ref[rows, pl.ds(v * 128, 128)], put(out_sq))
        spread(masked, put(out_fw))
        sides[rows, :] = outer_columns(sq_ref, rows)
        outer = jnp.where(outer_columns(holes_ref, rows) > 0, 0.0, outer_columns(fw_ref, rows))
        sides[pl.ds(pl.multiple_of(128 + brow * 8, 8), 8), :] = outer
        return carry

    for piece in range(4):
        for copy in copies[piece]:
            copy.wait()
        lax.fori_loop(piece * 4, piece * 4 + 4, tile_rows, 0, unroll=2)
    for edge, start in ((edge_up, 0), (edge_down, 112)):
        for part in range(2):
            rows = pl.ds(start + part * 8, 8)
            edge[pl.ds(part * 8, 8), :] = sq_ref[rows, :]
            edge[pl.ds(16 + part * 8, 8), :] = jnp.where(holes_ref[rows, :] > 0, 0.0, fw_ref[rows, :])


def rims_kernel(ok_ref, below_ref, above_ref, sides_ref, dens_ref, out_sq, out_fw, out_sides, out_dens):
    for field, out in ((0, out_sq), (1, out_fw)):
        for part in range(4):
            src = below_ref if part < 2 else above_ref
            ok = ok_ref[1] if part < 2 else ok_ref[0]
            rows = pl.ds(field * 16 + (part % 2) * 8, 8)

            def load(v, src=src, rows=rows, ok=ok):
                return jnp.where(ok > 0, src[rows, pl.ds(v * 128, 128)], 0.0)

            def store(c, x, part=part, out=out):
                out[pl.ds(c * 32 + part * 8, 8), :] = x

            spread(load, store)
            outer = jnp.where(ok > 0, outer_columns(src, rows), 0.0)
            out_sides[pl.ds(field * 160 + 128 + part * 8, 8), :] = outer
        out_sides[pl.ds(field * 160, 128), :] = sides_ref[pl.ds(field * 128, 128), :]
    out_dens[...] = dens_ref[...]


def filter_kernel(first_ref, got_ref, own_ref, tiles_ref, dens_ref, up_ref, down_ref, cols_ref,
                  slots, parts, prod, edge, first_block, sem):
    fetch = pltpu.make_async_copy(first_ref, first_block, sem)
    fetch.start()
    tiles = [tiles_ref[i].T for i in range(5)]
    inverse = inverse_denoms([jnp.sum(t, axis=0, keepdims=True) for t in tiles])
    weights = stacked(jnp.concatenate(tiles, axis=1))
    slots[pl.ds(0, SENT), :] = got_ref[...]
    slots[pl.ds(SENT, SLOTS), :] = own_ref[...]
    fetch.wait()
    offset = curve_offset(first_block[0])
    for brow in range(BROWS):
        x = jnp.concatenate(
            [slots[pl.ds(offset + inner_place(brow, g), 8, stride=256), :] for g in range(16)], axis=0
        )
        put_parts(parts, pl.ds(brow * 128, 128), x)
    for i in range(SLOTS // MROWS):
        rows = pl.ds(i * MROWS, MROWS)
        prod[rows, :] = jnp.dot(parts[rows, :], weights, preferred_element_type=jnp.float32)

    def part(k, brow):
        return lambda group: prod[pl.ds(brow * 128 + group * 8, 8), pl.ds(k * 128, 128)]

    for brow in range(BROWS):
        vecs = []
        for group in range(16):
            x = part(0, brow)(group)
            if brow > 0:
                x = x + part(1, brow - 1)(group)
            if brow < BROWS - 1:
                x = x + part(2, brow + 1)(group)
            x = x + from_left(part(3, brow), group)
            x = x + from_right(part(4, brow), group)
            vecs.append(x * inverse(brow, group))
        edge[pl.ds(0 * 16 + brow, 1), :] = vecs[0][0:1]
        edge[pl.ds(1 * 16 + brow, 1), :] = vecs[2][0:1]
        edge[pl.ds(2 * 16 + brow, 1), :] = vecs[13][7:8]
        edge[pl.ds(3 * 16 + brow, 1), :] = vecs[15][7:8]
        turned = jnp.concatenate(vecs, axis=0).T
        for a in range(8):
            dens_ref[pl.ds(a * QS * 16 + brow, 16, stride=16), :] = turned[a * 16:(a + 1) * 16]
        if brow == 0:
            up_ref[0:128, :] = turned
        if brow == 1:
            up_ref[128:256, :] = turned
        if brow == 2:
            up_ref[256:272, :] = turned[0:16]
        if brow == 13:
            down_ref[256:272, :] = turned[112:128]
        if brow == 14:
            down_ref[0:128, :] = turned
        if brow == 15:
            down_ref[128:256, :] = turned
    lane = lane_ids((16, 128))
    c0, c1, c126, c127 = (edge[pl.ds(i * 16, 16), :] for i in range(4))
    for a in range(8):
        x = jnp.where(lane < 16, roll(c0, -16 * a, 1), 0.0)
        x = jnp.where(lane == 16, roll(c1, 16 - 16 * a, 1), x)
        x = jnp.where(lane == 111, roll(c126, 96 - 16 * a, 1), x)
        x = jnp.where(lane >= 112, roll(c127, 112 - 16 * a, 1), x)
        cols_ref[pl.ds(a * 16, 16), :] = x


def corner_kernel(below_ref, above_ref, cols_ref, sides_ref, out_ref):
    out_ref[0:128, :] = cols_ref[...]
    out_ref[168:488, :] = sides_ref[...]
    lane = lane_ids()
    sub = sub_ids()
    for part in range(5):
        if part < 4:
            src = below_ref if part < 2 else above_ref

            def load(c, src=src, part=part):
                return src[pl.ds(c + (part % 2) * 128, 8, stride=16), :]
        else:

            def load(c):
                low = jnp.broadcast_to(below_ref[pl.ds(256 + c, 1), :], (8, 128))
                high = jnp.broadcast_to(above_ref[pl.ds(256 + c, 1), :], (8, 128))
                return jnp.where(sub == 0, low, high)

        x = jnp.zeros((8, 128), jnp.float32)
        for c in range(16):
            here = load(c)
            x = jnp.where(lane == c, roll(here, c, 1), x)
            x = jnp.where(lane == 112 + c, roll(here, c - 15, 1), x)
            if c == 0:
                x = jnp.where(lane == 16, here, x)
            if c == 15:
                x = jnp.where(lane == 111, here, x)
        out_ref[pl.ds(128 + part * 8, 8), :] = x


def solve_kernel(ok_ref, first_ref, dens_ref, below_ref, above_ref, left_ref, right_ref, sq_ref, fw_ref,
                 sq_rim, fw_rim, tiles_ref, p_out, back_ref, keep_ref,
                 k, far, wn, ws, we, ww, bp, ba, p0, p1, a0, a1, parts, prod, slots, first_block, sem):
    fetch = pltpu.make_async_copy(first_ref, first_block, sem)
    fetch.start()
    lane = lane_ids()
    sub = sub_ids()
    up_ok, down_ok, left_ok, right_ok = (ok_ref[i] > 0 for i in range(4))

    def conduct(d):
        return COND_FLOOR + (1.0 - COND_FLOOR) * d * d * d

    def fill(a, carry):
        for slot in range(16):
            for half in range(2):
                rows = pl.ds(pl.multiple_of((a * QS + slot) * 16 + half * 8, 8), 8)
                k[rows, :] = conduct(dens_ref[rows, :])
        return carry

    lax.fori_loop(0, 8, fill, 0)
    keep_right = (lane <= 16) & right_ok
    keep_left = (lane >= 111) & left_ok

    def side(rows):
        d = jnp.where(lane < 64, right_ref[rows, :], left_ref[rows, :])
        return jnp.where(keep_right | keep_left, conduct(d), 0.0)

    for a in range(8):
        for half in range(2):
            k[pl.ds(main_row(a, 16, half), 8), :] = side(pl.ds(a * 16 + half * 8, 8))
    for part in range(4):
        src, ok = (below_ref, down_ok) if part < 2 else (above_ref, up_ok)
        for slot in range(16):
            d = src[pl.ds(slot + (part % 2) * 128, 8, stride=16), :]
            k[pl.ds(rim_row(slot, part), 8), :] = jnp.where(ok, conduct(d), 0.0)
        k[pl.ds(rim_row(16, part), 8), :] = jnp.where(ok, side(pl.ds(128 + part * 8, 8)), 0.0)
    keep_far = ((sub == 0) & down_ok) | ((sub == 7) & up_ok)
    for slot in range(16):
        low = jnp.broadcast_to(below_ref[pl.ds(256 + slot, 1), :], (8, 128))
        high = jnp.broadcast_to(above_ref[pl.ds(256 + slot, 1), :], (8, 128))
        d = jnp.where(sub == 0, low, high)
        far[pl.ds(slot * 8, 8), :] = jnp.where(keep_far, conduct(d), 0.0)
    far[pl.ds(128, 8), :] = jnp.where(keep_far, side(pl.ds(160, 8)), 0.0)

    def vec(ref, base, row):
        if isinstance(base, int) and isinstance(row, int):
            return ref[pl.ds(base + row, 8), :]
        return ref[pl.ds(pl.multiple_of(base + row, 8), 8), :]

    def rows_at(row):
        return pl.ds(row if isinstance(row, int) else pl.multiple_of(row, 8), 8)

    def down_by_one(above, here):
        return jnp.where(sub == 0, roll(above, 1, 0), roll(here, 1, 0))

    def up_by_one(below, here):
        return jnp.where(sub == 7, roll(below, -1, 0), roll(here, -1, 0))

    def group(ref, base, a, half):
        ctr = [vec(ref, base, main_row(a, s, half)) for s in range(QS)]
        north, south = [], []
        for s in range(QS):
            if isinstance(a, int) and a == 0:
                if half == 0:
                    north.append(down_by_one(vec(ref, base, rim_row(s, 3)), vec(ref, base, main_row(7, s, 0))))
                else:
                    north.append(down_by_one(vec(ref, base, main_row(7, s, 0)), vec(ref, base, main_row(7, s, 1))))
            else:
                north.append(vec(ref, base, main_row(a - 1, s, half)))
            if isinstance(a, int) and a == 7:
                if half == 0:
                    south.append(up_by_one(vec(ref, base, main_row(0, s, 1)), vec(ref, base, main_row(0, s, 0))))
                else:
                    south.append(up_by_one(vec(ref, base, rim_row(s, 0)), vec(ref, base, main_row(0, s, 1))))
            else:
                south.append(vec(ref, base, main_row(a + 1, s, half)))
        return ctr, north, south

    def rim_group(ref, base, part, outer=None):
        ctr = [vec(ref, base, rim_row(s, part)) for s in range(QS)]
        north, south = [], []
        for s in range(QS):
            if part == 0:
                above = vec(ref, base, main_row(7, s, 1))
            elif part == 2:
                above = ctr[s] if outer is None else outer[pl.ds(s * 8, 8), :]
            else:
                above = vec(ref, base, rim_row(s, part - 1))
            if part == 3:
                below = vec(ref, base, main_row(0, s, 0))
            elif part == 1:
                below = ctr[s] if outer is None else outer[pl.ds(s * 8, 8), :]
            else:
                below = vec(ref, base, rim_row(s, part + 1))
            north.append(down_by_one(above, ctr[s]))
            south.append(up_by_one(below, ctr[s]))
        return ctr, north, south

    def each_group(body, parts):
        def inner(a, carry):
            for half in range(2):
                body(a, half, None)
            return carry

        lax.fori_loop(1, 7, inner, 0)
        for a in (0, 7):
            for half in range(2):
                body(a, half, None)
        for part in parts:
            body(None, None, part)

    def row_of(a, half, part, s):
        if part is not None:
            return rim_row(s, part)
        return main_row(a, s, half)

    def side_sources(a, half, part):
        for field in range(2):
            if part is None:
                rows = pl.ds(168 + field * 160 + half * 64 + a, 8, stride=8)
                ok = True
            else:
                rows = pl.ds(168 + field * 160 + 128 + part * 8, 8)
                ok = down_ok if part < 2 else up_ok
            x = jnp.where(lane < 64, right_ref[rows, :], left_ref[rows, :])
            yield jnp.where((keep_right | keep_left) & ok, x, 0.0)

    def coefficients(a, half, part):
        ctr, north, south = group(k, 0, a, half) if part is None else rim_group(k, 0, part, far)
        east, west = east_west(ctr)
        for s in range(QS):
            row = row_of(a, half, part, s)
            rows = pl.ds(row if isinstance(row, int) else pl.multiple_of(row, 8), 8)
            if s == 16:
                source, weight = side_sources(a, half, part)
            elif part is not None:
                here = pl.ds(s * 32 + part * 8, 8)
                source, weight = sq_rim[here, :], fw_rim[here, :]
            else:
                here = rows_at((a * 16 + s) * 16 + half * 8)
                source, weight = sq_ref[here, :], fw_ref[here, :]
            fn, fs, fe, fv = (0.5 * (ctr[s] + other[s]) for other in (north, south, east, west))
            inv = jnp.where(weight > 0.0, 1.0, 0.0) / (fn + fs + fv + fe + SQUEEZE_DAMPING)
            wn[rows, :] = fn * inv
            ws[rows, :] = fs * inv
            we[rows, :] = fe * inv
            ww[rows, :] = fv * inv
            first_p = source * inv
            first_a = weight * inv
            bp[rows, :] = first_p
            ba[rows, :] = first_a
            p0[rows, :] = first_p
            a0[rows, :] = first_a

    each_group(coefficients, range(4))

    def ends_of(ref, row):
        first, last, beside = (vec(ref, 0, row(s)) for s in (0, 15, 16))
        east, west = east_west([first] + [None] * 14 + [last, beside])
        return {15: east[15], 16: east[16]}, {0: west[0], 16: west[16]}

    def sweep(old, new, full):
        def relax(rows, neighbours):
            ends = [[ends_of(ref, row) for row in rows] for ref in old]
            before = [[None] * len(rows) for _ in old]
            here = [[vec(ref, 0, row(0)) for row in rows] for ref in old]
            for s in range(QS):
                after = [[vec(ref, 0, row(s + 1)) if s < QS - 1 else None for row in rows] for ref in old]
                around = [neighbours(f, s, here[f]) for f in range(2)]
                for i, row in enumerate(rows):
                    at = row(s)
                    cn, cs, ce, cw = (vec(c, 0, at) for c in (wn, ws, we, ww))
                    for f, start in enumerate((bp, ba)):
                        north, south = around[f][i]
                        east = ends[f][i][0].get(s, after[f][i])
                        west = ends[f][i][1].get(s, before[f][i])
                        x = (vec(start, 0, at) + cn * north) + (cs * south + (ce * east + cw * west))
                        new[f][rows_at(at), :] = x
                before, here = here, after

        def chunk(i, carry):
            a = CHUNK * i + 1
            for half in range(2):
                def neighbours(f, s, ctr, half=half):
                    north = vec(old[f], 0, main_row(a - 1, s, half))
                    south = vec(old[f], 0, main_row(a + CHUNK, s, half))
                    column = [north] + ctr + [south]
                    return [(column[j], column[j + 2]) for j in range(CHUNK)]

                relax([lambda s, half=half, j=j: main_row(a + j, s, half) for j in range(CHUNK)], neighbours)
            return carry

        if UNROLL:
            for i in range(6 // CHUNK):
                chunk(i, 0)
        else:
            lax.fori_loop(0, 6 // CHUNK, chunk, 0)

        ring = [
            lambda s: main_row(7, s, 0), lambda s: main_row(7, s, 1),
            lambda s: main_row(0, s, 0), lambda s: main_row(0, s, 1),
            lambda s: rim_row(s, 0), lambda s: rim_row(s, 3),
        ]
        if full:
            ring += [lambda s: rim_row(s, 1), lambda s: rim_row(s, 2)]

        def ring_neighbours(f, s, ctr):
            down = [roll(x, 1, 0) for x in ctr]
            up = [roll(x, -1, 0) for x in ctr]
            top, low = sub == 0, sub == 7
            ref = old[f]
            out = [
                (vec(ref, 0, main_row(6, s, 0)), jnp.where(low, up[3], up[2])),
                (vec(ref, 0, main_row(6, s, 1)), jnp.where(low, up[4], up[3])),
                (jnp.where(top, down[5], down[0]), vec(ref, 0, main_row(1, s, 0))),
                (jnp.where(top, down[0], down[1]), vec(ref, 0, main_row(1, s, 1))),
                (jnp.where(top, down[1], down[4]), jnp.where(low, up[6], up[4]) if full else up[4]),
                (jnp.where(top, down[7], down[5]) if full else down[5], jnp.where(low, up[2], up[5])),
            ]
            if full:
                out += [(jnp.where(top, down[4], down[6]), up[6]), (down[7], jnp.where(low, up[5], up[7]))]
            return out

        relax(ring, ring_neighbours)

    def two_sweeps(full):
        def step(i, carry):
            sweep((p0, a0), (p1, a1), full)
            sweep((p1, a1), (p0, a0), full)
            return carry

        return step

    lax.fori_loop(0, 4, two_sweeps(True), 0)
    lax.fori_loop(0, 3, two_sweeps(False), 0)
    sweep((p0, a0), (p1, a1), False)
    last = 0

    def gradient(a, half, part):
        p_c, p_n, p_s = group(p1, last, a, half)
        p_e, p_w = east_west(p_c)
        a_c, a_n, a_s = group(a1, last, a, half)
        a_e, a_w = east_west(a_c)
        for s in range(16):
            row = main_row(a, s, half)
            total = (a_c[s] - a_n[s]) * (p_c[s] - p_n[s])
            total = total + (a_c[s] - a_s[s]) * (p_c[s] - p_s[s])
            total = total + (a_c[s] - a_w[s]) * (p_c[s] - p_w[s])
            total = total + (a_c[s] - a_e[s]) * (p_c[s] - p_e[s])
            d = vec(dens_ref, 0, row)
            rows = pl.ds(row if isinstance(row, int) else pl.multiple_of(row, 8), 8)
            k[rows, :] = -0.5 * total * (3.0 * (1.0 - COND_FLOOR)) * d * d
            p_out[rows, :] = p_c[s]

    each_group(gradient, ())

    inverse = inverse_denoms([jnp.sum(tiles_ref[i].T, axis=0, keepdims=True) for i in range(5)])
    weights = stacked(jnp.concatenate([tiles_ref[i] for i in range(5)], axis=1))
    for brow in range(BROWS):
        film = jnp.concatenate(
            [k[pl.ds(a * QS * 16 + brow, 16, stride=16), :] for a in range(8)], axis=0
        ).T
        film = jnp.concatenate([film[g * 8:(g + 1) * 8] * inverse(brow, g) for g in range(16)], axis=0)
        put_parts(parts, pl.ds(brow * 128, 128), film)
    for i in range(SLOTS // MROWS):
        rows = pl.ds(i * MROWS, MROWS)
        prod[rows, :] = jnp.dot(parts[rows, :], weights, preferred_element_type=jnp.float32)

    def piece(i, brow):
        return lambda g: prod[pl.ds(brow * 128 + g * 8, 8), pl.ds(i * 128, 128)]

    fetch.wait()
    offset = curve_offset(first_block[0])
    for brow in range(BROWS):
        for g in range(16):
            x = piece(0, brow)(g)
            if brow < BROWS - 1:
                x = x + piece(1, brow + 1)(g)
            if brow > 0:
                x = x + piece(2, brow - 1)(g)
            x = x + from_right(piece(3, brow), g)
            x = x + from_left(piece(4, brow), g)
            slots[pl.ds(offset + inner_place(brow, g), 8, stride=256), :] = x
    back_ref[...] = slots[pl.ds(0, SENT), :]
    keep_ref[...] = slots[pl.ds(SENT, SLOTS), :]


def pressure_kernel(p_ref, out_ref):
    order = [column_of(i) for i in range(16)]

    def tile_rows(brow, carry):
        vecs = [p_ref[pl.ds(c * 16 + brow, 8, stride=QS * 16), :] for c in order]
        vecs = swap_stages(vecs)
        rows = pl.ds(pl.multiple_of(brow * 8, 8), 8)
        for v in range(16):
            out_ref[rows, pl.ds(v * 128, 128)] = vecs[v]
        return carry

    lax.fori_loop(0, BROWS, tile_rows, 0, unroll=4)


def moved(x, axis, by):
    length = lax.axis_size(axis)
    return lax.ppermute(x, axis, [(i, (i + by) % length) for i in range(length)])


def room(mib):
    return pltpu.CompilerParams(vmem_limit_bytes=mib * 1024 * 1024)


def work(flops, moved_bytes):
    return pl.CostEstimate(flops=flops, transcendentals=0, bytes_accessed=moved_bytes)


def f32(*shape):
    return jax.ShapeDtypeStruct(shape, jnp.float32)


def local(design, filter_tiles, filter_cols, slot_block, holes, squeeze_source, force_weight):
    smem = pl.BlockSpec(memory_space=pltpu.SMEM)
    vmem = pl.BlockSpec(memory_space=pltpu.VMEM)
    hbm = pl.BlockSpec(memory_space=pltpu.HBM)
    wide, narrow = lax.axis_index("wide"), lax.axis_index("narrow")
    inside = jnp.stack([
        wide > 0, wide < lax.axis_size("wide") - 1, narrow > 0, narrow < lax.axis_size("narrow") - 1,
    ]).astype(jnp.int32)
    tail, holes, squeeze_source, force_weight = lax.optimization_barrier(
        (design[SLOTS - SENT:], holes, squeeze_source, force_weight)
    )
    got = moved(tail, OWNERS, 1)
    sq, fw, sides, edge_up, edge_down = pl.pallas_call(
        sources_kernel,
        out_shape=(f32(SLOTS, 128), f32(SLOTS, 128), f32(256, 128), f32(32, 2048), f32(32, 2048)),
        in_specs=[hbm] * 3,
        scratch_shapes=[
            pltpu.VMEM((128, 2048), jnp.float32),
            pltpu.VMEM((128, 2048), jnp.float32),
            pltpu.VMEM((128, 2048), jnp.int32),
            pltpu.SemaphoreType.DMA((4, 3)),
        ],
        compiler_params=room(ROOM[0]),
        cost_estimate=work(2000000, 5500000),
        name="sources",
    )(*(pltpu.with_memory_space_constraint(x, pltpu.HBM) for x in (squeeze_source, force_weight, holes)))
    below = moved(edge_up, "wide", -1)
    above = moved(edge_down, "wide", 1)

    dens, up, down, cols = pl.pallas_call(
        filter_kernel,
        out_shape=(f32(MAIN, 128), f32(272, 128), f32(272, 128), f32(128, 128)),
        in_specs=[hbm, vmem, vmem, vmem],
        scratch_shapes=[
            pltpu.VMEM((SENT + SLOTS, 128), jnp.float32),
            pltpu.VMEM((SLOTS, 384), jnp.bfloat16),
            pltpu.VMEM((SLOTS, 640), jnp.float32),
            pltpu.VMEM((64, 128), jnp.float32),
            pltpu.SMEM((SLOTS,), jnp.int32),
            pltpu.SemaphoreType.DMA,
        ],
        compiler_params=room(ROOM[1]),
        cost_estimate=work(1100000000, 3500000),
        name="filter",
    )(slot_block, got, design, filter_tiles)
    d_below = moved(up, "wide", -1)
    d_above = moved(down, "wide", 1)
    below, above, cols = lax.optimization_barrier((below, above, cols))
    sq_rim, fw_rim, sides, dens = pl.pallas_call(
        rims_kernel,
        out_shape=(f32(512, 128), f32(512, 128), f32(320, 128), f32(MAIN, 128)),
        in_specs=[smem] + [vmem] * 4,
        compiler_params=room(ROOM[5]),
        cost_estimate=work(500000, 1200000),
        name="rims",
    )(inside, below, above, sides, dens)
    d_sides = pl.pallas_call(
        corner_kernel, out_shape=f32(488, 128), compiler_params=room(ROOM[2]),
        cost_estimate=work(200000, 700000), name="corners",
    )(d_below, d_above, cols, sides)
    d_right = moved(d_sides, "narrow", -1)
    d_left = moved(d_sides, "narrow", 1)

    big = pltpu.VMEM((EXT, 128), jnp.float32)
    p_film, back, keep = pl.pallas_call(
        solve_kernel,
        out_shape=(f32(MAIN, 128), f32(SENT, 128), f32(SLOTS, 128)),
        in_specs=[smem, hbm] + [vmem] * 10,
        scratch_shapes=[
            big, pltpu.VMEM((QS * 8, 128), jnp.float32), big, big, big, big, big, big, big, big, big, big,
            pltpu.VMEM((SLOTS, 384), jnp.bfloat16),
            pltpu.VMEM((SLOTS, 640), jnp.float32),
            pltpu.VMEM((SENT + SLOTS, 128), jnp.float32),
            pltpu.SMEM((SLOTS,), jnp.int32),
            pltpu.SemaphoreType.DMA,
        ],
        compiler_params=room(ROOM[3]),
        cost_estimate=work(1400000000, 9000000),
        name="solve",
    )(inside, slot_block, dens, d_below, d_above, d_left, d_right, sq, fw, sq_rim, fw_rim, filter_tiles)
    returned = moved(back, OWNERS, -1)
    pressure = pl.pallas_call(
        pressure_kernel, out_shape=f32(128, 2048), compiler_params=room(ROOM[4]), cost_estimate=work(2000000, 2100000), name="pressure",
    )(p_film)
    held = curve_offset(slot_block[0]) + (SLOTS - SENT)
    slot = lax.broadcasted_iota(jnp.int32, (SLOTS, 1), 0)
    upper = jnp.pad(returned, ((SLOTS - SENT, 0), (0, 0)))
    sensitivity = jnp.where(slot < held, keep, upper)
    return pressure, sensitivity


def solution(mesh):
    placed = (
        P(OWNERS, None),
        P(),
        P(OWNERS, None),
        P(OWNERS),
        P("wide", "narrow"),
        P("wide", "narrow"),
        P("wide", "narrow"),
    )
    return jax.shard_map(
        local,
        mesh=mesh,
        in_specs=placed,
        out_specs=(P("wide", "narrow"), P(OWNERS, None)),
        check_vma=False,
    )
```

```python
import jax
import jax.numpy as jnp
from jax import lax
from jax.experimental import pallas as pl
from jax.experimental.pallas import tpu as pltpu
from jax.sharding import PartitionSpec as P

SWEEPS = 16
CHUNK = 3
UNROLL = False
MROWS = 512
ROOM = (10, 11, 4, 30, 4, 4)
COND_FLOOR = 0.01
SQUEEZE_DAMPING = 0.25

SLOTS = 2048
SENT = 1536
BROWS = 16
QS = 17
MAIN = 8 * QS * 16
RIMS = QS * 32
EXT = MAIN + RIMS
OWNERS = ("wide", "narrow")


def main_row(a, slot, half):
    return (a * QS + slot) * 16 + half * 8


def rim_row(slot, part):
    return MAIN + slot * 32 + part * 8


def lane_ids(shape=(8, 128)):
    return lax.broadcasted_iota(jnp.int32, shape, 1)


def sub_ids(shape=(8, 128)):
    return lax.broadcasted_iota(jnp.int32, shape, 0)


def roll(x, by, axis):
    by = by % x.shape[axis]
    return x if by == 0 else pltpu.roll(x, by, axis)


def curve_offset(first_block):
    inner = first_block & (SLOTS - 1)
    row, col = inner >> 7, inner & 127
    h = (col >> 4) << 8
    for bit in range(4):
        h = h | (((col >> bit) & 1) << (2 * bit)) | (((row >> bit) & 1) << (2 * bit + 1))
    return SENT - h


def inner_place(brow, group):
    low, third = group >> 1, group & 1
    col = third * 8 + low
    place = 0
    for bit in range(4):
        place |= ((col >> bit) & 1) << (2 * bit)
        place |= ((brow >> bit) & 1) << (2 * bit + 1)
    return place


def swap_stages(vecs):
    lane = lane_ids(vecs[0].shape)
    vecs = list(vecs)
    for vec_bit, weight in ((0, 8), (3, 4), (2, 2), (1, 1)):
        upper = (lane & weight) != 0
        new = list(vecs)
        for i in range(16):
            if i & (1 << vec_bit):
                continue
            j = i | (1 << vec_bit)
            a, b = vecs[i], vecs[j]
            new[i] = jnp.where(upper, roll(b, weight, 1), a)
            new[j] = jnp.where(upper, b, roll(a, -weight, 1))
        vecs = new
    return vecs


def column_of(i):
    return ((i & 1) << 3) | (((i >> 3) & 1) << 2) | (((i >> 2) & 1) << 1) | ((i >> 1) & 1)


def east_west(ctr):
    lane = lane_ids()
    first, last, side = ctr[0], ctr[15], ctr[16]
    side_up, side_down = roll(side, 1, 1), roll(side, -1, 1)
    east15 = jnp.where(lane < 112, roll(first, -16, 1), roll(first, 104, 1))
    east15 = jnp.where(lane < 120, east15, roll(first, 119, 1))
    east15 = jnp.where(lane == 127, side_down, east15)
    west0 = jnp.where(lane >= 16, roll(last, 16, 1), roll(last, 24, 1))
    west0 = jnp.where(lane >= 8, west0, roll(last, 9, 1))
    west0 = jnp.where(lane == 0, side_up, west0)
    east16 = jnp.where(lane == 127, roll(first, -1, 1), side_down)
    west16 = jnp.where(lane == 0, roll(last, 1, 1), side_up)
    east = list(ctr[1:16]) + [east15, east16]
    west = [west0] + list(ctr[0:15]) + [west16]
    return east, west


def split(x):
    high = x.astype(jnp.bfloat16)
    low = (x - high.astype(jnp.float32)).astype(jnp.bfloat16)
    return high, low


def stacked(w):
    high, low = split(w)
    return jnp.concatenate([high, high, low], axis=0)


def put_parts(parts, rows, x):
    high, low = split(x)
    parts[rows, 0:128] = high
    parts[rows, 128:256] = low
    parts[rows, 256:384] = high


def inverse_denoms(sums):
    sub = sub_ids()
    table = {}
    for kind in range(3):
        base = sums[0]
        if kind != 0:
            base = base + sums[1]
        if kind != 2:
            base = base + sums[2]
        left = jnp.broadcast_to(sums[3], (8, 128))
        right = jnp.broadcast_to(sums[4], (8, 128))
        table[kind, 1] = 1.0 / (base + left + right)
        table[kind, 0] = 1.0 / (base + jnp.where(sub == 0, 0.0, left) + right)
        table[kind, 15] = 1.0 / (base + left + jnp.where(sub == 7, 0.0, right))

    def pick(brow, group):
        kind = 0 if brow == 0 else (2 if brow == BROWS - 1 else 1)
        return table[kind, group if group in (0, 15) else 1]

    return pick


def from_left(vecs, group):
    if group >= 2:
        return vecs(group - 2)
    if group == 1:
        return vecs(14)
    return jnp.where(sub_ids() == 0, 0.0, roll(vecs(15), 1, 0))


def from_right(vecs, group):
    if group < 14:
        return vecs(group + 2)
    if group == 14:
        return vecs(1)
    return jnp.where(sub_ids() == 7, 0.0, roll(vecs(0), -1, 0))


def spread(load, store):
    vecs = swap_stages([load(v) for v in range(16)])
    for i in range(16):
        store(column_of(i), vecs[i])


def outer_columns(ref, rows):
    return jnp.where(lane_ids() < 64, ref[rows, 0:128], ref[rows, 1920:2048])


def sources_kernel(sq_hbm, fw_hbm, holes_hbm, out_sq, sides, edge_up, edge_down,
                   sq_ref, fw_ref, holes_ref, sems):
    copies = []
    for piece in range(4):
        rows = pl.ds(piece * 32, 32)
        copies.append([
            pltpu.make_async_copy(src.at[rows, :], dst.at[rows, :], sems.at[piece, i])
            for i, (src, dst) in enumerate(((sq_hbm, sq_ref), (fw_hbm, fw_ref), (holes_hbm, holes_ref)))
        ])
        for copy in copies[-1]:
            copy.start()

    def tile_rows(brow, carry):
        rows = pl.ds(pl.multiple_of(brow * 8, 8), 8)

        def store(c, x):
            out_sq[pl.ds(c * 16 + brow, 8, stride=256), :] = x

        spread(lambda v: sq_ref[rows, pl.ds(v * 128, 128)], store)
        sides[rows, :] = outer_columns(sq_ref, rows)
        outer = jnp.where(outer_columns(holes_ref, rows) > 0, 0.0, outer_columns(fw_ref, rows))
        sides[pl.ds(pl.multiple_of(128 + brow * 8, 8), 8), :] = outer
        return carry

    for piece in range(4):
        for copy in copies[piece]:
            copy.wait()
        lax.fori_loop(piece * 4, piece * 4 + 4, tile_rows, 0, unroll=4)
    for edge, start in ((edge_up, 0), (edge_down, 112)):
        for part in range(2):
            rows = pl.ds(start + part * 8, 8)
            edge[pl.ds(part * 8, 8), :] = sq_ref[rows, :]
            edge[pl.ds(16 + part * 8, 8), :] = jnp.where(holes_ref[rows, :] > 0, 0.0, fw_ref[rows, :])


def weights_kernel(fw_hbm, holes_hbm, out_fw, fw_ref, holes_ref, sems):
    copies = []
    for piece in range(4):
        rows = pl.ds(piece * 32, 32)
        copies.append([
            pltpu.make_async_copy(src.at[rows, :], dst.at[rows, :], sems.at[piece, i])
            for i, (src, dst) in enumerate(((fw_hbm, fw_ref), (holes_hbm, holes_ref)))
        ])
        for copy in copies[-1]:
            copy.start()

    def tile_rows(brow, carry):
        rows = pl.ds(pl.multiple_of(brow * 8, 8), 8)

        def masked(v):
            cols = pl.ds(v * 128, 128)
            return jnp.where(holes_ref[rows, cols] > 0, 0.0, fw_ref[rows, cols])

        def store(c, x):
            out_fw[pl.ds(c * 16 + brow, 8, stride=256), :] = x

        spread(masked, store)
        return carry

    for piece in range(4):
        for copy in copies[piece]:
            copy.wait()
        lax.fori_loop(piece * 4, piece * 4 + 4, tile_rows, 0, unroll=4)


def rims_kernel(ok_ref, below_ref, above_ref, sides_ref, dens_ref, out_sq, out_fw, out_sides, out_dens):
    for field, out in ((0, out_sq), (1, out_fw)):
        for part in range(4):
            src = below_ref if part < 2 else above_ref
            ok = ok_ref[1] if part < 2 else ok_ref[0]
            rows = pl.ds(field * 16 + (part % 2) * 8, 8)

            def load(v, src=src, rows=rows, ok=ok):
                return jnp.where(ok > 0, src[rows, pl.ds(v * 128, 128)], 0.0)

            def store(c, x, part=part, out=out):
                out[pl.ds(c * 32 + part * 8, 8), :] = x

            spread(load, store)
            outer = jnp.where(ok > 0, outer_columns(src, rows), 0.0)
            out_sides[pl.ds(field * 160 + 128 + part * 8, 8), :] = outer
        out_sides[pl.ds(field * 160, 128), :] = sides_ref[pl.ds(field * 128, 128), :]
    out_dens[...] = dens_ref[...]


def filter_kernel(first_ref, got_ref, own_ref, tiles_ref, dens_ref, up_ref, down_ref, cols_ref,
                  slots, parts, prod, edge, first_block, sem):
    fetch = pltpu.make_async_copy(first_ref, first_block, sem)
    fetch.start()
    tiles = [tiles_ref[i].T for i in range(5)]
    inverse = inverse_denoms([jnp.sum(t, axis=0, keepdims=True) for t in tiles])
    weights = stacked(jnp.concatenate(tiles, axis=1))
    slots[pl.ds(0, SENT), :] = got_ref[...]
    slots[pl.ds(SENT, SLOTS), :] = own_ref[...]
    fetch.wait()
    offset = curve_offset(first_block[0])
    for brow in range(BROWS):
        x = jnp.concatenate(
            [slots[pl.ds(offset + inner_place(brow, g), 8, stride=256), :] for g in range(16)], axis=0
        )
        put_parts(parts, pl.ds(brow * 128, 128), x)
    for i in range(SLOTS // MROWS):
        rows = pl.ds(i * MROWS, MROWS)
        prod[rows, :] = jnp.dot(parts[rows, :], weights, preferred_element_type=jnp.float32)

    def part(k, brow):
        return lambda group: prod[pl.ds(brow * 128 + group * 8, 8), pl.ds(k * 128, 128)]

    for brow in range(BROWS):
        vecs = []
        for group in range(16):
            x = part(0, brow)(group)
            if brow > 0:
                x = x + part(1, brow - 1)(group)
            if brow < BROWS - 1:
                x = x + part(2, brow + 1)(group)
            x = x + from_left(part(3, brow), group)
            x = x + from_right(part(4, brow), group)
            vecs.append(x * inverse(brow, group))
        edge[pl.ds(0 * 16 + brow, 1), :] = vecs[0][0:1]
        edge[pl.ds(1 * 16 + brow, 1), :] = vecs[2][0:1]
        edge[pl.ds(2 * 16 + brow, 1), :] = vecs[13][7:8]
        edge[pl.ds(3 * 16 + brow, 1), :] = vecs[15][7:8]
        turned = jnp.concatenate(vecs, axis=0).T
        for a in range(8):
            dens_ref[pl.ds(a * QS * 16 + brow, 16, stride=16), :] = turned[a * 16:(a + 1) * 16]
        if brow == 0:
            up_ref[0:128, :] = turned
        if brow == 1:
            up_ref[128:256, :] = turned
        if brow == 2:
            up_ref[256:272, :] = turned[0:16]
        if brow == 13:
            down_ref[256:272, :] = turned[112:128]
        if brow == 14:
            down_ref[0:128, :] = turned
        if brow == 15:
            down_ref[128:256, :] = turned
    lane = lane_ids((16, 128))
    c0, c1, c126, c127 = (edge[pl.ds(i * 16, 16), :] for i in range(4))
    for a in range(8):
        x = jnp.where(lane < 16, roll(c0, -16 * a, 1), 0.0)
        x = jnp.where(lane == 16, roll(c1, 16 - 16 * a, 1), x)
        x = jnp.where(lane == 111, roll(c126, 96 - 16 * a, 1), x)
        x = jnp.where(lane >= 112, roll(c127, 112 - 16 * a, 1), x)
        cols_ref[pl.ds(a * 16, 16), :] = x


def corner_kernel(below_ref, above_ref, cols_ref, sides_ref, out_ref):
    out_ref[0:128, :] = cols_ref[...]
    out_ref[168:488, :] = sides_ref[...]
    lane = lane_ids()
    sub = sub_ids()
    for part in range(5):
        if part < 4:
            src = below_ref if part < 2 else above_ref

            def load(c, src=src, part=part):
                return src[pl.ds(c + (part % 2) * 128, 8, stride=16), :]
        else:

            def load(c):
                low = jnp.broadcast_to(below_ref[pl.ds(256 + c, 1), :], (8, 128))
                high = jnp.broadcast_to(above_ref[pl.ds(256 + c, 1), :], (8, 128))
                return jnp.where(sub == 0, low, high)

        x = jnp.zeros((8, 128), jnp.float32)
        for c in range(16):
            here = load(c)
            x = jnp.where(lane == c, roll(here, c, 1), x)
            x = jnp.where(lane == 112 + c, roll(here, c - 15, 1), x)
            if c == 0:
                x = jnp.where(lane == 16, here, x)
            if c == 15:
                x = jnp.where(lane == 111, here, x)
        out_ref[pl.ds(128 + part * 8, 8), :] = x


def solve_kernel(ok_ref, first_ref, dens_ref, below_ref, above_ref, left_ref, right_ref, sq_ref, fw_ref,
                 sq_rim, fw_rim, tiles_ref, p_out, back_ref, keep_ref,
                 k, far, wn, ws, we, ww, bp, ba, p0, p1, a0, a1, parts, prod, slots, first_block, sem):
    fetch = pltpu.make_async_copy(first_ref, first_block, sem)
    fetch.start()
    lane = lane_ids()
    sub = sub_ids()
    up_ok, down_ok, left_ok, right_ok = (ok_ref[i] > 0 for i in range(4))

    def conduct(d):
        return COND_FLOOR + (1.0 - COND_FLOOR) * d * d * d

    def fill(a, carry):
        for slot in range(16):
            for half in range(2):
                rows = pl.ds(pl.multiple_of((a * QS + slot) * 16 + half * 8, 8), 8)
                k[rows, :] = conduct(dens_ref[rows, :])
        return carry

    lax.fori_loop(0, 8, fill, 0)
    keep_right = (lane <= 16) & right_ok
    keep_left = (lane >= 111) & left_ok

    def side(rows):
        d = jnp.where(lane < 64, right_ref[rows, :], left_ref[rows, :])
        return jnp.where(keep_right | keep_left, conduct(d), 0.0)

    for a in range(8):
        for half in range(2):
            k[pl.ds(main_row(a, 16, half), 8), :] = side(pl.ds(a * 16 + half * 8, 8))
    for part in range(4):
        src, ok = (below_ref, down_ok) if part < 2 else (above_ref, up_ok)
        for slot in range(16):
            d = src[pl.ds(slot + (part % 2) * 128, 8, stride=16), :]
            k[pl.ds(rim_row(slot, part), 8), :] = jnp.where(ok, conduct(d), 0.0)
        k[pl.ds(rim_row(16, part), 8), :] = jnp.where(ok, side(pl.ds(128 + part * 8, 8)), 0.0)
    keep_far = ((sub == 0) & down_ok) | ((sub == 7) & up_ok)
    for slot in range(16):
        low = jnp.broadcast_to(below_ref[pl.ds(256 + slot, 1), :], (8, 128))
        high = jnp.broadcast_to(above_ref[pl.ds(256 + slot, 1), :], (8, 128))
        d = jnp.where(sub == 0, low, high)
        far[pl.ds(slot * 8, 8), :] = jnp.where(keep_far, conduct(d), 0.0)
    far[pl.ds(128, 8), :] = jnp.where(keep_far, side(pl.ds(160, 8)), 0.0)

    def vec(ref, base, row):
        if isinstance(base, int) and isinstance(row, int):
            return ref[pl.ds(base + row, 8), :]
        return ref[pl.ds(pl.multiple_of(base + row, 8), 8), :]

    def rows_at(row):
        return pl.ds(row if isinstance(row, int) else pl.multiple_of(row, 8), 8)

    def down_by_one(above, here):
        return jnp.where(sub == 0, roll(above, 1, 0), roll(here, 1, 0))

    def up_by_one(below, here):
        return jnp.where(sub == 7, roll(below, -1, 0), roll(here, -1, 0))

    def group(ref, base, a, half):
        ctr = [vec(ref, base, main_row(a, s, half)) for s in range(QS)]
        north, south = [], []
        for s in range(QS):
            if isinstance(a, int) and a == 0:
                if half == 0:
                    north.append(down_by_one(vec(ref, base, rim_row(s, 3)), vec(ref, base, main_row(7, s, 0))))
                else:
                    north.append(down_by_one(vec(ref, base, main_row(7, s, 0)), vec(ref, base, main_row(7, s, 1))))
            else:
                north.append(vec(ref, base, main_row(a - 1, s, half)))
            if isinstance(a, int) and a == 7:
                if half == 0:
                    south.append(up_by_one(vec(ref, base, main_row(0, s, 1)), vec(ref, base, main_row(0, s, 0))))
                else:
                    south.append(up_by_one(vec(ref, base, rim_row(s, 0)), vec(ref, base, main_row(0, s, 1))))
            else:
                south.append(vec(ref, base, main_row(a + 1, s, half)))
        return ctr, north, south

    def rim_group(ref, base, part, outer=None):
        ctr = [vec(ref, base, rim_row(s, part)) for s in range(QS)]
        north, south = [], []
        for s in range(QS):
            if part == 0:
                above = vec(ref, base, main_row(7, s, 1))
            elif part == 2:
                above = ctr[s] if outer is None else outer[pl.ds(s * 8, 8), :]
            else:
                above = vec(ref, base, rim_row(s, part - 1))
            if part == 3:
                below = vec(ref, base, main_row(0, s, 0))
            elif part == 1:
                below = ctr[s] if outer is None else outer[pl.ds(s * 8, 8), :]
            else:
                below = vec(ref, base, rim_row(s, part + 1))
            north.append(down_by_one(above, ctr[s]))
            south.append(up_by_one(below, ctr[s]))
        return ctr, north, south

    def each_group(body, parts):
        def inner(a, carry):
            for half in range(2):
                body(a, half, None)
            return carry

        lax.fori_loop(1, 7, inner, 0)
        for a in (0, 7):
            for half in range(2):
                body(a, half, None)
        for part in parts:
            body(None, None, part)

    def row_of(a, half, part, s):
        if part is not None:
            return rim_row(s, part)
        return main_row(a, s, half)

    def side_sources(a, half, part):
        for field in range(2):
            if part is None:
                rows = pl.ds(168 + field * 160 + half * 64 + a, 8, stride=8)
                ok = True
            else:
                rows = pl.ds(168 + field * 160 + 128 + part * 8, 8)
                ok = down_ok if part < 2 else up_ok
            x = jnp.where(lane < 64, right_ref[rows, :], left_ref[rows, :])
            yield jnp.where((keep_right | keep_left) & ok, x, 0.0)

    def coefficients(a, half, part):
        ctr, north, south = group(k, 0, a, half) if part is None else rim_group(k, 0, part, far)
        east, west = east_west(ctr)
        for s in range(QS):
            row = row_of(a, half, part, s)
            rows = pl.ds(row if isinstance(row, int) else pl.multiple_of(row, 8), 8)
            if s == 16:
                source, weight = side_sources(a, half, part)
            elif part is not None:
                here = pl.ds(s * 32 + part * 8, 8)
                source, weight = sq_rim[here, :], fw_rim[here, :]
            else:
                here = rows_at((a * 16 + s) * 16 + half * 8)
                source, weight = sq_ref[here, :], fw_ref[here, :]
            fn, fs, fe, fv = (0.5 * (ctr[s] + other[s]) for other in (north, south, east, west))
            inv = jnp.where(weight > 0.0, 1.0, 0.0) / (fn + fs + fv + fe + SQUEEZE_DAMPING)
            wn[rows, :] = fn * inv
            ws[rows, :] = fs * inv
            we[rows, :] = fe * inv
            ww[rows, :] = fv * inv
            first_p = source * inv
            first_a = weight * inv
            bp[rows, :] = first_p
            ba[rows, :] = first_a
            p0[rows, :] = first_p
            a0[rows, :] = first_a

    each_group(coefficients, range(4))

    def ends_of(ref, row):
        first, last, beside = (vec(ref, 0, row(s)) for s in (0, 15, 16))
        east, west = east_west([first] + [None] * 14 + [last, beside])
        return {15: east[15], 16: east[16]}, {0: west[0], 16: west[16]}

    def sweep(old, new, full):
        def relax(rows, neighbours):
            ends = [[ends_of(ref, row) for row in rows] for ref in old]
            before = [[None] * len(rows) for _ in old]
            here = [[vec(ref, 0, row(0)) for row in rows] for ref in old]
            for s in range(QS):
                after = [[vec(ref, 0, row(s + 1)) if s < QS - 1 else None for row in rows] for ref in old]
                around = [neighbours(f, s, here[f]) for f in range(2)]
                for i, row in enumerate(rows):
                    at = row(s)
                    cn, cs, ce, cw = (vec(c, 0, at) for c in (wn, ws, we, ww))
                    for f, start in enumerate((bp, ba)):
                        north, south = around[f][i]
                        east = ends[f][i][0].get(s, after[f][i])
                        west = ends[f][i][1].get(s, before[f][i])
                        x = (vec(start, 0, at) + cn * north) + (cs * south + (ce * east + cw * west))
                        new[f][rows_at(at), :] = x
                before, here = here, after

        def chunk(i, carry):
            a = CHUNK * i + 1
            for half in range(2):
                def neighbours(f, s, ctr, half=half):
                    north = vec(old[f], 0, main_row(a - 1, s, half))
                    south = vec(old[f], 0, main_row(a + CHUNK, s, half))
                    column = [north] + ctr + [south]
                    return [(column[j], column[j + 2]) for j in range(CHUNK)]

                relax([lambda s, half=half, j=j: main_row(a + j, s, half) for j in range(CHUNK)], neighbours)
            return carry

        if UNROLL:
            for i in range(6 // CHUNK):
                chunk(i, 0)
        else:
            lax.fori_loop(0, 6 // CHUNK, chunk, 0)

        ring = [
            lambda s: main_row(7, s, 0), lambda s: main_row(7, s, 1),
            lambda s: main_row(0, s, 0), lambda s: main_row(0, s, 1),
            lambda s: rim_row(s, 0), lambda s: rim_row(s, 3),
        ]
        if full:
            ring += [lambda s: rim_row(s, 1), lambda s: rim_row(s, 2)]

        def ring_neighbours(f, s, ctr):
            down = [roll(x, 1, 0) for x in ctr]
            up = [roll(x, -1, 0) for x in ctr]
            top, low = sub == 0, sub == 7
            ref = old[f]
            out = [
                (vec(ref, 0, main_row(6, s, 0)), jnp.where(low, up[3], up[2])),
                (vec(ref, 0, main_row(6, s, 1)), jnp.where(low, up[4], up[3])),
                (jnp.where(top, down[5], down[0]), vec(ref, 0, main_row(1, s, 0))),
                (jnp.where(top, down[0], down[1]), vec(ref, 0, main_row(1, s, 1))),
                (jnp.where(top, down[1], down[4]), jnp.where(low, up[6], up[4]) if full else up[4]),
                (jnp.where(top, down[7], down[5]) if full else down[5], jnp.where(low, up[2], up[5])),
            ]
            if full:
                out += [(jnp.where(top, down[4], down[6]), up[6]), (down[7], jnp.where(low, up[5], up[7]))]
            return out

        relax(ring, ring_neighbours)

    def two_sweeps(full):
        def step(i, carry):
            sweep((p0, a0), (p1, a1), full)
            sweep((p1, a1), (p0, a0), full)
            return carry

        return step

    lax.fori_loop(0, 4, two_sweeps(True), 0)
    lax.fori_loop(0, 3, two_sweeps(False), 0)
    sweep((p0, a0), (p1, a1), False)
    last = 0

    def gradient(a, half, part):
        p_c, p_n, p_s = group(p1, last, a, half)
        p_e, p_w = east_west(p_c)
        a_c, a_n, a_s = group(a1, last, a, half)
        a_e, a_w = east_west(a_c)
        for s in range(16):
            row = main_row(a, s, half)
            total = (a_c[s] - a_n[s]) * (p_c[s] - p_n[s])
            total = total + (a_c[s] - a_s[s]) * (p_c[s] - p_s[s])
            total = total + (a_c[s] - a_w[s]) * (p_c[s] - p_w[s])
            total = total + (a_c[s] - a_e[s]) * (p_c[s] - p_e[s])
            d = vec(dens_ref, 0, row)
            rows = pl.ds(row if isinstance(row, int) else pl.multiple_of(row, 8), 8)
            k[rows, :] = -0.5 * total * (3.0 * (1.0 - COND_FLOOR)) * d * d
            p_out[rows, :] = p_c[s]

    each_group(gradient, ())

    inverse = inverse_denoms([jnp.sum(tiles_ref[i].T, axis=0, keepdims=True) for i in range(5)])
    weights = stacked(jnp.concatenate([tiles_ref[i] for i in range(5)], axis=1))
    for brow in range(BROWS):
        film = jnp.concatenate(
            [k[pl.ds(a * QS * 16 + brow, 16, stride=16), :] for a in range(8)], axis=0
        ).T
        film = jnp.concatenate([film[g * 8:(g + 1) * 8] * inverse(brow, g) for g in range(16)], axis=0)
        put_parts(parts, pl.ds(brow * 128, 128), film)
    for i in range(SLOTS // MROWS):
        rows = pl.ds(i * MROWS, MROWS)
        prod[rows, :] = jnp.dot(parts[rows, :], weights, preferred_element_type=jnp.float32)

    def piece(i, brow):
        return lambda g: prod[pl.ds(brow * 128 + g * 8, 8), pl.ds(i * 128, 128)]

    fetch.wait()
    offset = curve_offset(first_block[0])
    for brow in range(BROWS):
        for g in range(16):
            x = piece(0, brow)(g)
            if brow < BROWS - 1:
                x = x + piece(1, brow + 1)(g)
            if brow > 0:
                x = x + piece(2, brow - 1)(g)
            x = x + from_right(piece(3, brow), g)
            x = x + from_left(piece(4, brow), g)
            slots[pl.ds(offset + inner_place(brow, g), 8, stride=256), :] = x
    back_ref[...] = slots[pl.ds(0, SENT), :]
    keep_ref[...] = slots[pl.ds(SENT, SLOTS), :]


def pressure_kernel(p_ref, out_ref):
    order = [column_of(i) for i in range(16)]

    def tile_rows(brow, carry):
        vecs = [p_ref[pl.ds(c * 16 + brow, 8, stride=QS * 16), :] for c in order]
        vecs = swap_stages(vecs)
        rows = pl.ds(pl.multiple_of(brow * 8, 8), 8)
        for v in range(16):
            out_ref[rows, pl.ds(v * 128, 128)] = vecs[v]
        return carry

    lax.fori_loop(0, BROWS, tile_rows, 0, unroll=4)


def moved(x, axis, by):
    length = lax.axis_size(axis)
    return lax.ppermute(x, axis, [(i, (i + by) % length) for i in range(length)])


def room(mib):
    return pltpu.CompilerParams(vmem_limit_bytes=mib * 1024 * 1024)


def work(flops, moved_bytes):
    return pl.CostEstimate(flops=flops, transcendentals=0, bytes_accessed=moved_bytes)


def f32(*shape):
    return jax.ShapeDtypeStruct(shape, jnp.float32)


def local(design, filter_tiles, filter_cols, slot_block, holes, squeeze_source, force_weight):
    smem = pl.BlockSpec(memory_space=pltpu.SMEM)
    vmem = pl.BlockSpec(memory_space=pltpu.VMEM)
    hbm = pl.BlockSpec(memory_space=pltpu.HBM)
    wide, narrow = lax.axis_index("wide"), lax.axis_index("narrow")
    inside = jnp.stack([
        wide > 0, wide < lax.axis_size("wide") - 1, narrow > 0, narrow < lax.axis_size("narrow") - 1,
    ]).astype(jnp.int32)
    tail, holes, squeeze_source, force_weight = lax.optimization_barrier(
        (design[SLOTS - SENT:], holes, squeeze_source, force_weight)
    )
    got = moved(tail, OWNERS, 1)
    sq, sides, edge_up, edge_down = pl.pallas_call(
        sources_kernel,
        out_shape=(f32(SLOTS, 128), f32(256, 128), f32(32, 2048), f32(32, 2048)),
        in_specs=[hbm] * 3,
        scratch_shapes=[
            pltpu.VMEM((128, 2048), jnp.float32),
            pltpu.VMEM((128, 2048), jnp.float32),
            pltpu.VMEM((128, 2048), jnp.int32),
            pltpu.SemaphoreType.DMA((4, 3)),
        ],
        compiler_params=room(ROOM[0]),
        cost_estimate=work(2000000, 5500000),
        name="sources",
    )(*(pltpu.with_memory_space_constraint(x, pltpu.HBM) for x in (squeeze_source, force_weight, holes)))
    below = moved(edge_up, "wide", -1)
    above = moved(edge_down, "wide", 1)

    dens, up, down, cols = pl.pallas_call(
        filter_kernel,
        out_shape=(f32(MAIN, 128), f32(272, 128), f32(272, 128), f32(128, 128)),
        in_specs=[hbm, vmem, vmem, vmem],
        scratch_shapes=[
            pltpu.VMEM((SENT + SLOTS, 128), jnp.float32),
            pltpu.VMEM((SLOTS, 384), jnp.bfloat16),
            pltpu.VMEM((SLOTS, 640), jnp.float32),
            pltpu.VMEM((64, 128), jnp.float32),
            pltpu.SMEM((SLOTS,), jnp.int32),
            pltpu.SemaphoreType.DMA,
        ],
        compiler_params=room(ROOM[1]),
        cost_estimate=work(1100000000, 3500000),
        name="filter",
    )(slot_block, got, design, filter_tiles)
    d_below = moved(up, "wide", -1)
    d_above = moved(down, "wide", 1)
    below, above, cols = lax.optimization_barrier((below, above, cols))
    sq_rim, fw_rim, sides, dens = pl.pallas_call(
        rims_kernel,
        out_shape=(f32(512, 128), f32(512, 128), f32(320, 128), f32(MAIN, 128)),
        in_specs=[smem] + [vmem] * 4,
        compiler_params=room(ROOM[5]),
        cost_estimate=work(500000, 1200000),
        name="rims",
    )(inside, below, above, sides, dens)
    d_sides = pl.pallas_call(
        corner_kernel, out_shape=f32(488, 128), compiler_params=room(ROOM[2]),
        cost_estimate=work(200000, 700000), name="corners",
    )(d_below, d_above, cols, sides)
    d_sides, force_weight, holes = lax.optimization_barrier((d_sides, force_weight, holes))
    fw = pl.pallas_call(
        weights_kernel,
        out_shape=f32(SLOTS, 128),
        in_specs=[hbm] * 2,
        scratch_shapes=[
            pltpu.VMEM((128, 2048), jnp.float32),
            pltpu.VMEM((128, 2048), jnp.int32),
            pltpu.SemaphoreType.DMA((4, 2)),
        ],
        compiler_params=room(ROOM[0]),
        cost_estimate=work(1000000, 3000000),
        name="weights",
    )(*(pltpu.with_memory_space_constraint(x, pltpu.HBM) for x in (force_weight, holes)))
    d_right = moved(d_sides, "narrow", -1)
    d_left = moved(d_sides, "narrow", 1)

    big = pltpu.VMEM((EXT, 128), jnp.float32)
    p_film, back, keep = pl.pallas_call(
        solve_kernel,
        out_shape=(f32(MAIN, 128), f32(SENT, 128), f32(SLOTS, 128)),
        in_specs=[smem, hbm] + [vmem] * 10,
        scratch_shapes=[
            big, pltpu.VMEM((QS * 8, 128), jnp.float32), big, big, big, big, big, big, big, big, big, big,
            pltpu.VMEM((SLOTS, 384), jnp.bfloat16),
            pltpu.VMEM((SLOTS, 640), jnp.float32),
            pltpu.VMEM((SENT + SLOTS, 128), jnp.float32),
            pltpu.SMEM((SLOTS,), jnp.int32),
            pltpu.SemaphoreType.DMA,
        ],
        compiler_params=room(ROOM[3]),
        cost_estimate=work(1400000000, 9000000),
        name="solve",
    )(inside, slot_block, dens, d_below, d_above, d_left, d_right, sq, fw, sq_rim, fw_rim, filter_tiles)
    returned = moved(back, OWNERS, -1)
    pressure = pl.pallas_call(
        pressure_kernel, out_shape=f32(128, 2048), compiler_params=room(ROOM[4]), cost_estimate=work(2000000, 2100000), name="pressure",
    )(p_film)
    held = curve_offset(slot_block[0]) + (SLOTS - SENT)
    slot = lax.broadcasted_iota(jnp.int32, (SLOTS, 1), 0)
    upper = jnp.pad(returned, ((SLOTS - SENT, 0), (0, 0)))
    sensitivity = jnp.where(slot < held, keep, upper)
    return pressure, sensitivity


def solution(mesh):
    placed = (
        P(OWNERS, None),
        P(),
        P(OWNERS, None),
        P(OWNERS),
        P("wide", "narrow"),
        P("wide", "narrow"),
        P("wide", "narrow"),
    )
    return jax.shard_map(
        local,
        mesh=mesh,
        in_specs=placed,
        out_specs=(P("wide", "narrow"), P(OWNERS, None)),
        check_vma=False,
    )
```
